256 devices in a mesh: tile: 32 (over y, z), curve: 8 (over x, core).
Axes of the slice: x: 4, y: 4, z: 8, core: 2. Of those that a mesh axis runs over, the one named last changes fastest.
Arguments:
- points: bfloat16 [32, 1024, 512], P('tile', 'curve'), may hold values from -6 to 6
- valid_rows: int32 [32, 8], P('tile', 'curve'), may hold values from 32 to 128, as said below
- dest_shard: int32 [32, 8, 1], P('tile', 'curve'), may hold values from 0 to 7, as said below
- dest_slot: int32 [32, 8, 1], P('tile', 'curve'), may hold values from 0 to 0, as said below
- norm_gain: float32 [2, 512], replicated, may hold values from 0.1 to 1.9
- w_xz: bfloat16 [2, 512, 2048], replicated, may hold values from -0.25 to 0.25
- w_bc: bfloat16 [2, 512, 256], replicated, may hold values from -0.25 to 0.25
- w_dt: bfloat16 [2, 512, 16], replicated, may hold values from -0.25 to 0.25
- dt_bias: float32 [2, 16], replicated, may hold values from -1 to 1
- decay_rate: float32 [2, 16], replicated, may hold values from 9.155273e-07 to 0.1
- skip_gain: float32 [2, 16], replicated, may hold values from 0.5 to 1.5
- gate_gain: float32 [2, 1024], replicated, may hold values from 0.1 to 1.9
- w_out: bfloat16 [2, 1024, 512], replicated, may hold values from -0.1875 to 0.1875
Outputs:
- mixed: bfloat16 [32, 1024, 512], P('tile', 'curve')
The draws below stay inside these ranges and needn't reach their ends.
Inputs may be any that keep to these rules, and one draw needn't show every extreme that they name: `valid_rows`: every tile has a curve shard with all 128 points live. `dest_shard`: within each tile, the 1 block of a curve shard go to 1 different curve shards, and every curve shard receives 1 block, one for each slot. `dest_slot`: together with dest_shard, every slot of every curve shard is filled exactly once.
All inputs are finite; a program needn't handle non-finite values.
Results may differ from the reference program's by a relative error of at most 0.0061.
Values may be sent and summed in bfloat16 or wider, within the bound.
A program may use at most 320 MiB of HBM per device.

```python
import math
import jax
import jax.numpy as jnp
from jax import lax

D = 512
H = 16
S = 128
LAYERS = 2
ROWS_DEV = 128
BLOCK = 128
E = 1024
BLOCKS = 1
CURVES = 8
TILES = 32
TILE_ROWS = 1024
N_CURVE = 8


def draw_valid_rows(key, part):
    count_key, full_key = jax.random.split(key, 2)
    counts = jax.random.randint(count_key, (TILES, CURVES), ROWS_DEV // 4, ROWS_DEV + 1)
    fullest = jax.random.randint(full_key, (TILES,), 0, CURVES)
    shard_index = lax.iota(jnp.int32, CURVES)
    return jnp.where(shard_index[None, :] == fullest[:, None], ROWS_DEV, counts).astype(jnp.int32)


def block_routing(key):
    base_key = jax.random.fold_in(key, 17)

    def one_tile(tile_key):
        tile_keys = jax.random.split(tile_key, 4)
        shuffle = jax.random.permutation(tile_keys[0], CURVES)
        shifts = jax.random.permutation(tile_keys[1], CURVES)[:BLOCKS]
        local_order = jax.vmap(lambda sub_key: jax.random.permutation(sub_key, BLOCKS))(jax.random.split(tile_keys[2], CURVES))
        slot_order = jax.vmap(lambda sub_key: jax.random.permutation(sub_key, BLOCKS))(jax.random.split(tile_keys[3], CURVES))
        source = lax.iota(jnp.int32, CURVES)[:, None]
        target = shuffle[(source + shifts[local_order]) % CURVES]
        slot_ids = slot_order[target, local_order]
        return (target.astype(jnp.int32), slot_ids.astype(jnp.int32))
    return jax.vmap(one_tile)(jax.random.split(base_key, TILES))


def draw_dest_shard(key, part):
    return block_routing(key)[0]


def draw_dest_slot(key, part):
    return block_routing(key)[1]


def draw_decay_rate(key, part):
    lengths = jnp.array([ROWS_DEV * CURVES, ROWS_DEV * CURVES * TILES], jnp.float32)
    pick_key, slow_key, fast_key, middle_key = jax.random.split(key, 4)
    ranking = jax.vmap(lambda sub_key: jax.random.permutation(sub_key, H))(jax.random.split(pick_key, LAYERS))
    layer_index = lax.iota(jnp.int32, LAYERS)[:, None]
    slow_count = jnp.where(layer_index == 0, H // 2, 0)
    middle_count = jnp.where(layer_index == 0, H // 4, H - H // 4)
    slow_heads = ranking < slow_count
    middle_heads = ranking < slow_count + middle_count
    slow_rate = jnp.exp(jax.random.uniform(slow_key, (LAYERS, H), jnp.float32, jnp.log(0.03), jnp.log(0.5))) / lengths[:, None]
    middle_low = jnp.where(layer_index == 0, math.log(0.5), math.log(0.13))
    middle_high = jnp.where(layer_index == 0, math.log(2.0), math.log(0.26))
    middle_spread = jax.random.uniform(middle_key, (LAYERS, H), jnp.float32)
    middle_rate = jnp.exp(middle_low + middle_spread * (middle_high - middle_low)) / ROWS_DEV
    fast_rate = jnp.exp(jax.random.uniform(fast_key, (LAYERS, H), jnp.float32, jnp.log(0.02), jnp.log(0.1)))
    return jnp.where(slow_heads, slow_rate, jnp.where(middle_heads, middle_rate, fast_rate)).astype(jnp.float32)


def block_scale(stream_key, extent, cuts, low, top_value):
    def one(position, blocks):
        steps = jax.random.uniform(jax.random.fold_in(jax.random.fold_in(stream_key, 6), position), (blocks,), jnp.float32, low / len(cuts), top_value / len(cuts))
        return jnp.repeat(jnp.exp(steps), extent[position] // blocks).reshape((-1,) + (1,) * (len(extent) - position - 1))

    factor_of = one(*cuts[0])
    for cut in cuts[1:]:
        factor_of = factor_of * one(*cut)
    return factor_of


def centred(stream_key, shape, deviation, bound, cuts=(), kind=jnp.bfloat16):
    values = jax.random.normal(stream_key, shape, jnp.float32) * deviation
    if len(cuts) > 0:
        values = block_scale(stream_key, shape, cuts, -0.22, 0.18) * values
    return jnp.clip(values, min=-bound, max=bound).astype(kind)


def setup_inputs(seed: int = 0) -> dict:
    splits = jax.random.split(jax.random.key(seed), 14)
    points = centred(splits[0], (TILES, TILE_ROWS, D), 1.0, 6.0, ((0, 32), (1, 8)))
    valid_rows = draw_valid_rows(jax.random.fold_in(splits[13], 71), 0)
    dest_shard = draw_dest_shard(jax.random.fold_in(splits[13], 71), 0)
    dest_slot = draw_dest_slot(jax.random.fold_in(splits[13], 71), 0)
    norm_gain = jnp.clip(1.0 + 0.18 * jax.random.normal(splits[4], (LAYERS, D), jnp.float32), 0.1, 1.9)
    w_xz = centred(splits[5], (LAYERS, D, 2 * E), D ** -0.5, 0.25)
    w_bc = centred(splits[6], (LAYERS, D, 2 * S), D ** -0.5, 0.25)
    w_dt = centred(splits[7], (LAYERS, D, H), D ** -0.5, 0.25)
    dt_bias = jnp.clip(jax.random.uniform(splits[8], (LAYERS, H), jnp.float32, -1.0, 1.0), -1.0, 1.0)
    decay_rate = draw_decay_rate(jax.random.fold_in(splits[13], 71), 0)
    skip_gain = jnp.clip(jax.random.uniform(splits[10], (LAYERS, H), jnp.float32, 0.5, 1.5), 0.5, 1.5)
    gate_gain = jnp.clip(1.0 + 0.18 * jax.random.normal(splits[11], (LAYERS, E), jnp.float32), 0.1, 1.9)
    w_out = centred(splits[12], (LAYERS, E, D), E ** -0.5, 0.1875)
    return dict(points=points, valid_rows=valid_rows, dest_shard=dest_shard, dest_slot=dest_slot, norm_gain=norm_gain, w_xz=w_xz, w_bc=w_bc, w_dt=w_dt, dt_bias=dt_bias, decay_rate=decay_rate, skip_gain=skip_gain, gate_gain=gate_gain, w_out=w_out)


highest = lax.Precision.HIGHEST

def prepare(inputs, live_rows, norm_g, proj_xz, proj_bc, proj_dt, shift_dt, rate_dt):
    widened = inputs.astype(jnp.float32)
    scaled = widened * lax.rsqrt(lax.optimization_barrier(jnp.mean(widened * widened, axis=-1, keepdims=True)) + 1e-05) * norm_g
    normed = scaled.astype(jnp.bfloat16)
    joined = jnp.dot(normed, proj_xz, preferred_element_type=jnp.float32)
    inner_width = joined.shape[1] // 2
    values = jax.nn.silu(joined[:, :inner_width]).astype(jnp.bfloat16)
    gate_pre = joined[:, inner_width:]
    mixed_bc = jnp.dot(normed, proj_bc, preferred_element_type=jnp.float32)
    state_width = mixed_bc.shape[1] // 2
    key_rows = jax.nn.silu(mixed_bc[:, :state_width]).astype(jnp.bfloat16)
    query_rows = jax.nn.silu(mixed_bc[:, state_width:]).astype(jnp.bfloat16)
    step_sizes = jax.nn.softplus(jnp.dot(normed, proj_dt, preferred_element_type=jnp.float32) + shift_dt) * live_rows[:, None]
    running = jnp.cumsum(-step_sizes * rate_dt, axis=0)
    log_total = running[-1]
    head_count = step_sizes.shape[1]
    head_values = values.astype(jnp.float32).reshape(values.shape[0], head_count, -1)
    to_end = jnp.exp(log_total[None, :] - running) * step_sizes
    end_state = jnp.einsum('shp,sn->hpn', head_values * to_end[:, :, None], key_rows.astype(jnp.float32), precision=highest)
    return ((log_total, end_state), (widened, gate_pre, key_rows, query_rows, step_sizes, running, head_values))

def finish(carried, pieces, skip_g, gate_g, proj_out, live_rows):
    widened, gate_pre, key_rows, query_rows, step_sizes, running, head_values = pieces
    row_count = widened.shape[0]
    block_rows = min(512, row_count)
    running_heads = running.T
    steps_heads = step_sizes.T
    outputs = []
    for first_row in range(0, row_count, block_rows):
        last_row = first_row + block_rows
        scores = jnp.dot(query_rows[first_row:last_row], key_rows[:last_row].T, preferred_element_type=jnp.float32)
        causal = (first_row + lax.iota(jnp.int32, block_rows))[:, None] >= lax.iota(jnp.int32, last_row)[None, :]
        gaps = running_heads[:, first_row:last_row, None] - running_heads[:, None, :last_row]
        weights = jnp.where(causal[None], jnp.exp(jnp.where(causal[None], gaps, 0.0)), 0.0)
        weights = weights * steps_heads[:, None, :last_row] * scores[None]
        inside = jnp.einsum('hts,shp->thp', weights, head_values[:last_row], precision=highest)
        from_state = jnp.einsum('hpn,tn->thp', carried, query_rows[first_row:last_row].astype(jnp.float32), precision=highest)
        carried_part = jnp.exp(running[first_row:last_row])[:, :, None] * from_state
        outputs.append(inside + carried_part + skip_g[None, :, None] * head_values[first_row:last_row])
    head_out = jnp.concatenate(outputs, axis=0).reshape(row_count, -1)
    gated = head_out * jax.nn.silu(gate_pre)
    normed = (gated * lax.rsqrt(lax.optimization_barrier(jnp.mean(gated * gated, axis=-1, keepdims=True)) + 1e-05) * gate_g).astype(jnp.bfloat16)
    update = jnp.dot(normed, proj_out, preferred_element_type=jnp.float32)
    return (widened + live_rows[:, None] * update).astype(jnp.bfloat16)

def run_chain(shards, live, layer, params):
    norm_gain, w_xz, w_bc, w_dt, dt_bias, decay_rate, skip_gain, gate_gain, w_out = params
    head_count = w_dt.shape[-1]
    head_size = w_xz.shape[-1] // 2 // head_count
    state_width = w_bc.shape[-1] // 2
    start_state = jnp.zeros((head_count, head_size, state_width), jnp.float32)

    def advance(carried, item_pair):
        summary, pieces = prepare(item_pair[0], item_pair[1], norm_gain[layer], w_xz[layer], w_bc[layer], w_dt[layer], dt_bias[layer], decay_rate[layer])
        layer_out = finish(carried, pieces, skip_gain[layer], gate_gain[layer], w_out[layer], item_pair[1])
        return (jnp.exp(summary[0])[:, None, None] * carried + summary[1], layer_out)
    final_state, outputs = lax.scan(advance, start_state, (shards, live))
    return outputs

def reference(points, valid_rows, dest_shard, dest_slot, norm_gain, w_xz, w_bc, w_dt, dt_bias, decay_rate, skip_gain, gate_gain, w_out):
    params = (norm_gain, w_xz, w_bc, w_dt, dt_bias, decay_rate, skip_gain, gate_gain, w_out)
    tile_count = points.shape[0]
    model_width = points.shape[2]
    row_index = jnp.arange(ROWS_DEV, dtype=jnp.int32)
    live_first = (row_index[None, None, :] < valid_rows[:, :, None]).astype(jnp.float32)
    shards = points.reshape(tile_count, N_CURVE, ROWS_DEV, model_width)

    def one_tile(tile_item):
        return run_chain(tile_item[0], tile_item[1], 0, params)
    first = lax.map(one_tile, (shards, live_first))
    blocks = first.reshape(tile_count, N_CURVE * BLOCKS, BLOCK * model_width)
    block_index = jnp.arange(BLOCKS, dtype=jnp.int32) * BLOCK
    block_live = jnp.clip(valid_rows[:, :, None] - block_index[None, None, :], 0, BLOCK).reshape(tile_count, -1)
    target = (dest_shard * BLOCKS + dest_slot).reshape(tile_count, -1).astype(jnp.int32)

    def place_rows(tile_blocks, tile_target):
        return jnp.zeros_like(tile_blocks).at[tile_target].set(tile_blocks)
    moved = jax.vmap(place_rows)(blocks, target)
    moved_live = jax.vmap(place_rows)(block_live, target)
    live_second = (jnp.arange(BLOCK, dtype=jnp.int32)[None, None, :] < moved_live[:, :, None]).astype(jnp.float32)
    live_second = live_second.reshape(tile_count * N_CURVE, ROWS_DEV)
    second = run_chain(moved.reshape(tile_count * N_CURVE, ROWS_DEV, model_width), live_second, 1, params)
    return second.reshape(tile_count, N_CURVE * ROWS_DEV, model_width)
```

```python
import functools

import jax
import jax.numpy as jnp
from jax import lax
from jax.experimental import pallas as pl
from jax.experimental.pallas import tpu as pltpu
from jax.sharding import PartitionSpec as P

F32 = jnp.float32
BF16 = jnp.bfloat16
HI = lax.Precision.HIGHEST
NC = 8
R = 128
D = 512
E = 1024
H = 16
CH = 512


def silu(v):
    return v * jax.nn.sigmoid(v)


def softplus(v):
    return jnp.maximum(v, 0.0) + jnp.log1p(jnp.exp(-jnp.abs(v)))


def mesh_copy(src, dst, send_sem, recv_sem, tile, curve):
    return pltpu.make_async_remote_copy(
        src_ref=src,
        dst_ref=dst,
        send_sem=send_sem,
        recv_sem=recv_sem,
        device_id=(tile, curve),
        device_id_type=pl.DeviceIdType.MESH,
    )


def kernel(
    NY,
    NZ,
    valid_s,
    dest_s,
    x_h,
    ng_h,
    wxz_h,
    wbc_h,
    wdt_h,
    dtb_h,
    rate_h,
    skip_h,
    gg_h,
    wout_h,
    out_h,
    x_v,
    ng,
    wxz,
    wbc,
    wdt,
    dtb,
    rate,
    skip,
    gg,
    wout,
    in_sem,
    exp_m,
    vals,
    gate,
    inner,
    decx,
    sA,
    rA,
    lS,
    lR,
    sC,
    rC,
    pre,
    lpre,
    sB1,
    rB1,
    sB2,
    rB2,
    sB3,
    rB3,
    mS,
    mR,
    pS,
    pR,
    out_v,
    a_send,
    a_recv,
    l_send,
    l_recv,
    c_send,
    c_recv,
    b1_send,
    b1_recv,
    b2_send,
    b2_recv,
    b3_send,
    b3_recv,
    m_send,
    m_recv,
    out_sem,
):
    t = lax.axis_index("tile")
    c = lax.axis_index("curve")
    y = t // NZ
    z = lax.rem(t, NZ)
    RZ = R // NZ
    curve_peer = [lax.rem(c + k, NC) for k in range(NC)]
    z_peer = [lax.rem(z + k, NZ) for k in range(NZ)]
    y_peer = [lax.rem(y + k, NY) for k in range(NY)]

    barrier = pltpu.get_barrier_semaphore()

    def hello(tile, curve):
        pl.semaphore_signal(
            barrier, inc=1, device_id=(tile, curve), device_id_type=pl.DeviceIdType.MESH
        )

    for k in range(1, NC):
        hello(t, curve_peer[k])
    for k in range(1, NZ):
        hello(y * NZ + z_peer[k], c)
    for k in range(1, NY):
        hello(y_peer[k] * NZ + z, c)

    n_in = [0]

    def fetch(src, dst):
        cp = pltpu.make_async_copy(src, dst, in_sem.at[n_in[0]])
        n_in[0] += 1
        cp.start()
        return cp

    x_cp = fetch(x_h.at[0], x_v)
    small_cp = [
        fetch(a, b)
        for a, b in ((ng_h, ng), (dtb_h, dtb), (rate_h, rate), (skip_h, skip), (gg_h, gg))
    ]
    dt_cp = [fetch(wdt_h.at[0], wdt.at[0])]
    bc_cp = [fetch(wbc_h.at[0], wbc.at[0])]

    def fetch_xz(layer):
        return [
            fetch(wxz_h.at[layer, :, pl.ds(q * CH, CH)], wxz.at[layer, q])
            for q in range(2 * E // CH)
        ]

    xz_cp = [fetch_xz(0)]
    out_cp = [fetch(wout_h.at[0], wout.at[0])]

    lane = lax.broadcasted_iota(jnp.int32, (R, R), 1)
    row = lax.broadcasted_iota(jnp.int32, (R, R), 0)
    row_f = row.astype(F32)
    causal = row >= lane
    tri = jnp.where(causal, 1.0, 0.0).astype(F32)
    erow = lax.broadcasted_iota(jnp.int32, (R, E), 0)
    ecol = lax.broadcasted_iota(jnp.int32, (R, E), 1)
    exp_m[...] = jnp.where(
        jnp.logical_and(erow < 48, (erow & 15) == (ecol >> 6)), 1.0, 0.0
    ).astype(BF16)
    rep = jnp.where(
        lax.broadcasted_iota(jnp.int32, (H, R), 0)
        == (lax.broadcasted_iota(jnp.int32, (H, R), 1) & 15),
        1.0,
        0.0,
    )
    rep_b = rep.astype(BF16)

    def widen(v):
        hi = v.astype(BF16).astype(F32)
        rest = v - hi
        mid = rest.astype(BF16).astype(F32)
        low = rest - mid
        ln = lax.broadcasted_iota(jnp.int32, v.shape, 1)
        parts = jnp.where(ln < 16, hi, jnp.where(ln < 32, mid, low)).astype(BF16)
        return jnp.dot(parts, exp_m[...], preferred_element_type=F32)

    def copies8(v):
        return jnp.dot(v, rep, precision=HI, preferred_element_type=F32)

    x_cp.wait()
    for cp in small_cp:
        cp.wait()
    bias8, rate8, skip8 = copies8(dtb[...]), copies8(rate[...]), copies8(skip[...])
    skip_x = widen(jnp.concatenate([skip8] * 4, axis=0))

    valid_row = jnp.full((1, R), valid_s[0, 0], jnp.int32).astype(F32)
    dest_row = jnp.full((1, R), dest_s[0, 0, 0], jnp.int32).astype(F32)

    def norm_of(xb, layer):
        w = xb.astype(F32)
        ms = jnp.mean(w * w, axis=-1, keepdims=True)
        return (w * lax.rsqrt(ms + 1e-05) * ng[layer : layer + 1, :]).astype(BF16)

    def times_of(nb, live, layer):
        wrep = jnp.dot(wdt[layer], rep_b, preferred_element_type=F32).astype(BF16)
        steps = softplus(
            jnp.dot(nb, wrep, preferred_element_type=F32) + bias8[layer : layer + 1, :]
        )
        steps = steps * live
        running = jnp.dot(
            tri, -steps * rate8[layer : layer + 1, :], precision=HI, preferred_element_type=F32
        )
        return steps, running

    def project_values(nb, layer):
        for q in range(E // CH):
            v = jnp.dot(nb, wxz[layer, q], preferred_element_type=F32)
            vals[:, q * CH : (q + 1) * CH] = silu(v).astype(BF16)

    def project_gate(nb, layer):
        for q in range(E // CH):
            v = jnp.dot(nb, wxz[layer, q + E // CH], preferred_element_type=F32)
            gate[:, q * CH : (q + 1) * CH] = silu(v)

    def keys_of(nb, layer):
        return silu(jnp.dot(nb, wbc[layer, :, 0:R], preferred_element_type=F32))

    def queries_of(nb, layer):
        return silu(jnp.dot(nb, wbc[layer, :, R : 2 * R], preferred_element_type=F32)).astype(BF16)

    def summary(layer, steps, running, keys):
        total = running[R - 1 : R, :]
        wide = widen(jnp.exp(total - running) * steps)
        keys_t = keys.T.astype(BF16)
        for j in range(NC):
            cols = slice(j * R, (j + 1) * R)
            scaled = (vals[:, cols].astype(F32) * wide[:, cols]).astype(BF16)
            sA[layer, j] = jnp.dot(keys_t, scaled, preferred_element_type=F32).astype(BF16)
        total_x = widen(jnp.broadcast_to(total, (8, R)))
        for j in range(NC):
            lS[layer, j : j + 1, :] = total_x[0:1, j * R : (j + 1) * R]
        if layer == 0:
            lS[layer, 8:16, :] = jnp.concatenate(
                [dest_row, valid_row, jnp.zeros((6, R), F32)], axis=0
            )
        else:
            lS[layer, 8:16, :] = jnp.zeros((8, R), F32)

    sent = []

    def send_summary(layer):
        got = []
        for k in range(1, NC):
            cp = mesh_copy(
                lS.at[layer],
                lR.at[layer, c],
                l_send.at[layer, k],
                l_recv.at[layer, k],
                t,
                curve_peer[k],
            )
            cp.start()
            got.append(cp)
            cp = mesh_copy(
                sA.at[layer, curve_peer[k]],
                rA.at[layer, c],
                a_send.at[layer, k],
                a_recv.at[layer, k],
                t,
                curve_peer[k],
            )
            cp.start()
            got.append(cp)
        lR[layer, c] = lS[layer]
        rA[layer, c] = sA[layer, c]
        sent.extend(got)
        return got

    def arrive(copies):
        for cp in copies:
            cp.wait_recv()

    def chain(layer):
        logs = [lR[layer, s, pl.ds(c, 1), :] for s in range(NC)]
        if layer == 0:
            place = [jnp.full((1, R), float(s), F32) for s in range(NC)]
        else:
            place = [lR[0, s, 8:9, :] for s in range(NC)]

        def lap(p, carry):
            state, log_sum = carry
            if layer == 0:
                sC[0, p] = state.astype(BF16)
            else:
                pre[p] = state
                lpre[p] = jnp.broadcast_to(log_sum, (8, R))
            pf = p.astype(F32)
            here = [jnp.where(place[s] == pf, 1.0, 0.0) for s in range(NC)]
            log_p = here[0] * logs[0]
            new = here[0] * rA[layer, 0].astype(F32)
            for s in range(1, NC):
                log_p = log_p + here[s] * logs[s]
                new = new + here[s] * rA[layer, s].astype(F32)
            return jnp.exp(log_p) * state + new, log_sum + log_p

        return lax.fori_loop(0, NC, lap, (jnp.zeros((R, R), F32), jnp.zeros((1, R), F32)))

    def send_carried(layer):
        got = []
        for k in range(1, NC):
            cp = mesh_copy(
                sC.at[layer, curve_peer[k]],
                rC.at[layer, c],
                c_send.at[layer, k],
                c_recv.at[layer, k],
                t,
                curve_peer[k],
            )
            cp.start()
            got.append(cp)
        rC[layer, c] = sC[layer, c]
        sent.extend(got)
        return got

    def inside(layer, steps, running, keys, queries):
        scores = lax.dot_general(
            queries, keys.astype(BF16), (((1,), (1,)), ((), ())), preferred_element_type=F32
        )
        scores = jnp.where(causal, scores, 0.0)
        running_t = running.T
        steps_t = steps.T
        half = lane < 64
        decx[...] = widen(jnp.exp(running))

        for j in range(NC):
            cols = slice(j * R, (j + 1) * R)
            v = vals[:, cols]
            vf = v.astype(F32)
            acc = skip_x[layer : layer + 1, cols] * vf
            for e in range(2):
                h = 2 * j + e
                gap = running[:, h : h + 1] - running_t[h : h + 1, :]
                w = jnp.exp(jnp.minimum(gap, 0.0)) * steps_t[h : h + 1, :] * scores
                ve = jnp.where(half if e == 0 else jnp.logical_not(half), vf, 0.0)
                acc = acc + jnp.dot(w.astype(BF16), ve.astype(BF16), preferred_element_type=F32)
            inner[:, cols] = acc

    def finish(layer, xb, live_col, queries):
        squares = jnp.zeros((R, R), F32)
        for j in range(NC):
            cols = slice(j * R, (j + 1) * R)
            from_state = jnp.dot(queries, rC[layer, j], preferred_element_type=F32)
            g = (inner[:, cols] + decx[:, cols] * from_state) * gate[:, cols]
            squares = squares + g * g
            inner[:, cols] = g
        scale = lax.rsqrt(jnp.sum(squares, axis=-1, keepdims=True) * (1.0 / E) + 1e-05)
        scaled = (inner[...] * scale * gg[layer : layer + 1, :]).astype(BF16)
        update = jnp.dot(scaled, wout[layer], preferred_element_type=F32)
        return (xb.astype(F32) + live_col * update).astype(BF16)

    xb = x_v[...]
    live = jnp.where(row_f < valid_row, 1.0, 0.0)
    nb = norm_of(xb, 0)
    dt_cp[0].wait()
    steps, running = times_of(nb, live, 0)
    bc_cp[0].wait()
    keys = keys_of(nb, 0)
    xz_cp[0][0].wait()
    xz_cp[0][1].wait()
    project_values(nb, 0)
    summary(0, steps, running, keys)
    pl.semaphore_wait(barrier, (NC - 1) + (NZ - 1) + (NY - 1))
    got = send_summary(0)
    dt_cp.append(fetch(wdt_h.at[1], wdt.at[1]))
    bc_cp.append(fetch(wbc_h.at[1], wbc.at[1]))
    xz_cp.append(fetch_xz(1))
    out_cp.append(fetch(wout_h.at[1], wout.at[1]))
    xz_cp[0][2].wait()
    xz_cp[0][3].wait()
    project_gate(nb, 0)
    queries = queries_of(nb, 0)
    arrive(got)
    chain(0)
    got = send_carried(0)
    inside(0, steps, running, keys, queries)
    out_cp[0].wait()
    arrive(got)
    first = finish(0, xb, live[:, 0:1], queries)
    mS[...] = first

    nb = norm_of(first, 1)
    dt_cp[1].wait()
    steps, running = times_of(nb, live, 1)
    bc_cp[1].wait()
    keys = keys_of(nb, 1)
    for cp in xz_cp[1]:
        cp.wait()
    out_cp[1].wait()
    project_values(nb, 1)
    summary(1, steps, running, keys)
    got_a = send_summary(1)

    got_m = []
    for k in range(1, 4):
        cp = mesh_copy(
            mS, mR.at[k], m_send.at[k], m_recv.at[k], t, lax.rem(c + 2 * k, NC)
        )
        cp.start()
        got_m.append(cp)
    sent.extend(got_m)

    arrive(got_a)
    tile_state, tile_log = chain(1)
    for k in range(NZ):
        sB1[k, 0:RZ, :] = tile_state[k * RZ : (k + 1) * RZ, :]
        sB1[k, RZ : RZ + 8, :] = jnp.broadcast_to(tile_log, (8, R))
    got = []
    for k in range(1, NZ):
        cp = mesh_copy(
            sB1.at[z_peer[k]],
            rB1.at[z],
            b1_send.at[k],
            b1_recv.at[k],
            y * NZ + z_peer[k],
            c,
        )
        cp.start()
        got.append(cp)
    rB1[z] = sB1[z]
    sent.extend(got)
    arrive(got)

    state = jnp.zeros((RZ, R), F32)
    log_sum = jnp.zeros((1, R), F32)
    row_states, row_logs = [], []
    for k in range(NZ):
        row_states.append(state)
        row_logs.append(log_sum)
        log_k = rB1[k, RZ : RZ + 1, :]
        state = jnp.exp(log_k) * state + rB1[k, 0:RZ, :]
        log_sum = log_sum + log_k
    sB2[0:RZ, :] = state
    sB2[RZ : RZ + 8, :] = jnp.broadcast_to(log_sum, (8, R))
    got = []
    for k in range(1, NY):
        cp = mesh_copy(
            sB2, rB2.at[y], b2_send.at[k], b2_recv.at[k], y_peer[k] * NZ + z, c
        )
        cp.start()
        got.append(cp)
    rB2[y] = sB2[...]
    sent.extend(got)

    arrive(got_m)
    partner = c + 1 - 2 * lax.rem(c, 2)
    c_f, partner_f = c.astype(F32), partner.astype(F32)
    mine = jnp.zeros((R, D), F32)
    theirs = jnp.zeros((R, D), F32)
    for k in range(4):
        src = lax.rem(c + NC - 2 * k, NC)
        goes = lR[0, src, 8:9, :]
        blk = (first if k == 0 else mR[k]).astype(F32)
        m_mine = jnp.concatenate([jnp.where(goes == c_f, 1.0, 0.0)] * 4, axis=1)
        m_theirs = jnp.concatenate([jnp.where(goes == partner_f, 1.0, 0.0)] * 4, axis=1)
        mine = mine + m_mine * blk
        theirs = theirs + m_theirs * blk
    pS[...] = theirs.astype(BF16)
    swap = mesh_copy(pS, pR, m_send.at[0], m_recv.at[0], t, partner)
    swap.start()
    sent.append(swap)
    valid_row = jnp.zeros((1, R), F32)
    for s in range(NC):
        valid_row = valid_row + jnp.where(lR[0, s, 8:9, :] == c_f, 1.0, 0.0) * lR[0, s, 9:10, :]
    live = jnp.where(row_f < valid_row, 1.0, 0.0)

    arrive(got)
    state = jnp.zeros((RZ, R), F32)
    for k in range(NY):
        new = jnp.exp(rB2[k, RZ : RZ + 1, :]) * state + rB2[k, 0:RZ, :]
        state = jnp.where(k < y, new, state)
    for k in range(NZ):
        sB3[k] = (jnp.exp(row_logs[k]) * state + row_states[k]).astype(BF16)
    got = []
    for k in range(1, NZ):
        cp = mesh_copy(
            sB3.at[z_peer[k]],
            rB3.at[z],
            b3_send.at[k],
            b3_recv.at[k],
            y * NZ + z_peer[k],
            c,
        )
        cp.start()
        got.append(cp)
    rB3[z] = sB3[z]
    sent.extend(got)

    swap.wait_recv()
    xb = (mine + pR[...].astype(F32)).astype(BF16)
    nb = norm_of(xb, 1)
    steps, running = times_of(nb, live, 1)
    keys = keys_of(nb, 1)
    queries = queries_of(nb, 1)
    project_values(nb, 1)

    arrive(got)
    entry = jnp.concatenate([rB3[k].astype(F32) for k in range(NZ)], axis=0)
    for p in range(NC):
        sC[1, p] = (jnp.exp(lpre[p, 0:1, :]) * entry + pre[p]).astype(BF16)
    got = send_carried(1)
    project_gate(nb, 1)
    inside(1, steps, running, keys, queries)
    arrive(got)
    out_v[...] = finish(1, xb, live[:, 0:1], queries)
    done = pltpu.make_async_copy(out_v, out_h.at[0], out_sem)
    done.start()
    for cp in sent:
        cp.wait_send()
    done.wait()


def call(NY, NZ, points, valid_rows, dest_shard, *params):
    RZ = R // NZ
    V = pltpu.VMEM
    DMA = pltpu.SemaphoreType.DMA
    any_spec = pl.BlockSpec(memory_space=pl.ANY)
    smem = pl.BlockSpec(memory_space=pltpu.SMEM)
    return pl.pallas_call(
        functools.partial(kernel, NY, NZ),
        out_shape=jax.ShapeDtypeStruct(points.shape, points.dtype),
        in_specs=[smem, smem] + [any_spec] * 10,
        out_specs=any_spec,
        scratch_shapes=[
            V((R, D), BF16),
            V((2, D), F32),
            V((2, 2 * E // CH, D, CH), BF16),
            V((2, D, 2 * R), BF16),
            V((2, D, H), BF16),
            V((2, H), F32),
            V((2, H), F32),
            V((2, H), F32),
            V((2, E), F32),
            V((2, E, D), BF16),
            DMA((20,)),
            V((R, E), BF16),
            V((R, E), BF16),
            V((R, E), F32),
            V((R, E), F32),
            V((R, E), F32),
            V((2, NC, R, R), BF16),
            V((2, NC, R, R), BF16),
            V((2, 16, R), F32),
            V((2, NC, 16, R), F32),
            V((2, NC, R, R), BF16),
            V((2, NC, R, R), BF16),
            V((NC, R, R), F32),
            V((NC, 8, R), F32),
            V((NZ, RZ + 8, R), F32),
            V((NZ, RZ + 8, R), F32),
            V((RZ + 8, R), F32),
            V((NY, RZ + 8, R), F32),
            V((NZ, RZ, R), BF16),
            V((NZ, RZ, R), BF16),
            V((R, D), BF16),
            V((4, R, D), BF16),
            V((R, D), BF16),
            V((R, D), BF16),
            V((R, D), BF16),
            DMA((2, NC)),
            DMA((2, NC)),
            DMA((2, NC)),
            DMA((2, NC)),
            DMA((2, NC)),
            DMA((2, NC)),
            DMA((NZ,)),
            DMA((NZ,)),
            DMA((NY,)),
            DMA((NY,)),
            DMA((NZ,)),
            DMA((NZ,)),
            DMA((4,)),
            DMA((4,)),
            DMA(()),
        ],
        compiler_params=pltpu.CompilerParams(
            collective_id=0, has_side_effects=True, vmem_limit_bytes=48 * 1024 * 1024
        ),
    )(valid_rows, dest_shard, points, *params)


def solution(mesh):
    tiles = mesh.shape["tile"]
    NZ = min(8, max(1, tiles // 2))
    NY = tiles // NZ

    def local(points, valid_rows, dest_shard, dest_slot, *params):
        return call(NY, NZ, points, valid_rows, dest_shard, *params)

    in_specs = (
        P("tile", "curve", None),
        P("tile", "curve"),
        P("tile", "curve", None),
        P("tile", "curve", None),
    ) + (P(),) * 9
    return jax.shard_map(
        local, mesh=mesh, in_specs=in_specs, out_specs=P("tile", "curve", None), check_vma=False
    )
```

```python
import functools

import jax
import jax.numpy as jnp
from jax import lax
from jax.experimental import pallas as pl
from jax.experimental.pallas import tpu as pltpu
from jax.sharding import PartitionSpec as P

F32 = jnp.float32
BF16 = jnp.bfloat16
HI = lax.Precision.HIGHEST
NC = 8
R = 128
D = 512
E = 1024
H = 16
CH = 512


def silu(v):
    return v * jax.nn.sigmoid(v)


def softplus(v):
    return jnp.maximum(v, 0.0) + jnp.log1p(jnp.exp(-jnp.abs(v)))


def mesh_copy(src, dst, send_sem, recv_sem, tile, curve):
    return pltpu.make_async_remote_copy(
        src_ref=src,
        dst_ref=dst,
        send_sem=send_sem,
        recv_sem=recv_sem,
        device_id=(tile, curve),
        device_id_type=pl.DeviceIdType.MESH,
    )


def kernel(
    NY,
    NZ,
    valid_s,
    dest_s,
    x_h,
    ng_h,
    wxz_h,
    wbc_h,
    wdt_h,
    dtb_h,
    rate_h,
    skip_h,
    gg_h,
    wout_h,
    out_h,
    x_v,
    ng,
    wxz,
    wbc,
    wdt,
    dtb,
    rate,
    skip,
    gg,
    wout,
    in_sem,
    exp_m,
    vals,
    gate,
    inner,
    decx,
    sA,
    rA,
    lS,
    lR,
    sC,
    rC,
    pre,
    lpre,
    sB1,
    rB1,
    sB2,
    rB2,
    sB3,
    rB3,
    mS,
    mR,
    pS,
    pR,
    out_v,
    a_send,
    a_recv,
    l_send,
    l_recv,
    c_send,
    c_recv,
    b1_send,
    b1_recv,
    b2_send,
    b2_recv,
    b3_send,
    b3_recv,
    m_send,
    m_recv,
    out_sem,
):
    t = lax.axis_index("tile")
    c = lax.axis_index("curve")
    y = t // NZ
    z = lax.rem(t, NZ)
    RZ = R // NZ
    curve_peer = [lax.rem(c + k, NC) for k in range(NC)]
    z_peer = [lax.rem(z + k, NZ) for k in range(NZ)]
    y_peer = [lax.rem(y + k, NY) for k in range(NY)]

    barrier = pltpu.get_barrier_semaphore()

    def hello(tile, curve):
        pl.semaphore_signal(
            barrier, inc=1, device_id=(tile, curve), device_id_type=pl.DeviceIdType.MESH
        )

    for k in range(1, NC):
        hello(t, curve_peer[k])
    for k in range(1, NZ):
        hello(y * NZ + z_peer[k], c)
    for k in range(1, NY):
        hello(y_peer[k] * NZ + z, c)

    n_in = [0]

    def fetch(src, dst):
        cp = pltpu.make_async_copy(src, dst, in_sem.at[n_in[0]])
        n_in[0] += 1
        cp.start()
        return cp

    x_cp = fetch(x_h.at[0], x_v)
    small_cp = [
        fetch(a, b)
        for a, b in ((ng_h, ng), (dtb_h, dtb), (rate_h, rate), (skip_h, skip), (gg_h, gg))
    ]
    dt_cp = [fetch(wdt_h.at[0], wdt.at[0])]
    bc_cp = [fetch(wbc_h.at[0], wbc.at[0])]

    def fetch_xz(layer):
        return [
            fetch(wxz_h.at[layer, :, pl.ds(q * CH, CH)], wxz.at[layer, q])
            for q in range(2 * E // CH)
        ]

    xz_cp = [fetch_xz(0)]
    out_cp = [fetch(wout_h.at[0], wout.at[0])]

    lane = lax.broadcasted_iota(jnp.int32, (R, R), 1)
    row = lax.broadcasted_iota(jnp.int32, (R, R), 0)
    row_f = row.astype(F32)
    causal = row >= lane
    tri = jnp.where(causal, 1.0, 0.0).astype(F32)
    erow = lax.broadcasted_iota(jnp.int32, (R, E), 0)
    ecol = lax.broadcasted_iota(jnp.int32, (R, E), 1)
    exp_m[...] = jnp.where(
        jnp.logical_and(erow < 48, (erow & 15) == (ecol >> 6)), 1.0, 0.0
    ).astype(BF16)
    rep = jnp.where(
        lax.broadcasted_iota(jnp.int32, (H, R), 0)
        == (lax.broadcasted_iota(jnp.int32, (H, R), 1) & 15),
        1.0,
        0.0,
    )

    def widen(v):
        hi = v.astype(BF16).astype(F32)
        rest = v - hi
        mid = rest.astype(BF16).astype(F32)
        low = rest - mid
        ln = lax.broadcasted_iota(jnp.int32, v.shape, 1)
        parts = jnp.where(ln < 16, hi, jnp.where(ln < 32, mid, low)).astype(BF16)
        return jnp.dot(parts, exp_m[...], preferred_element_type=F32)

    def copies8(v):
        return jnp.dot(v, rep, precision=HI, preferred_element_type=F32)

    x_cp.wait()
    for cp in small_cp:
        cp.wait()
    bias8, rate8, skip8 = copies8(dtb[...]), copies8(rate[...]), copies8(skip[...])
    skip_x = widen(jnp.concatenate([skip8] * 4, axis=0))

    valid_row = jnp.full((1, R), valid_s[0, 0], jnp.int32).astype(F32)
    dest_row = jnp.full((1, R), dest_s[0, 0, 0], jnp.int32).astype(F32)

    def norm_of(xb, layer):
        w = xb.astype(F32)
        ms = jnp.mean(w * w, axis=-1, keepdims=True)
        return (w * lax.rsqrt(ms + 1e-05) * ng[layer : layer + 1, :]).astype(BF16)

    def times_of(nb, live, layer):
        wrep = jnp.concatenate([wdt[layer]] * 8, axis=0)
        raw = lax.dot_general(
            nb, wrep, (((1,), (1,)), ((), ())), preferred_element_type=F32
        )
        steps = softplus(raw + bias8[layer : layer + 1, :])
        steps = steps * live
        running = jnp.dot(
            tri, -steps * rate8[layer : layer + 1, :], precision=HI, preferred_element_type=F32
        )
        return steps, running

    def project_values(nb, layer):
        for q in range(E // CH):
            v = jnp.dot(nb, wxz[layer, q], preferred_element_type=F32)
            vals[:, q * CH : (q + 1) * CH] = silu(v).astype(BF16)

    def project_gate(nb, layer):
        for q in range(E // CH):
            v = jnp.dot(nb, wxz[layer, q + E // CH], preferred_element_type=F32)
            gate[:, q * CH : (q + 1) * CH] = silu(v)

    def keys_of(nb, layer):
        return silu(jnp.dot(nb, wbc[layer, :, 0:R], preferred_element_type=F32))

    def queries_of(nb, layer):
        return silu(jnp.dot(nb, wbc[layer, :, R : 2 * R], preferred_element_type=F32)).astype(BF16)

    def summary(layer, steps, running, keys):
        total = running[R - 1 : R, :]
        wide = widen(jnp.exp(total - running) * steps)
        keys_t = keys.T.astype(BF16)
        for j in range(NC):
            cols = slice(j * R, (j + 1) * R)
            scaled = (vals[:, cols].astype(F32) * wide[:, cols]).astype(BF16)
            sA[layer, j] = jnp.dot(keys_t, scaled, preferred_element_type=F32).astype(BF16)
        total_x = widen(jnp.broadcast_to(total, (8, R)))
        for j in range(NC):
            lS[layer, j : j + 1, :] = total_x[0:1, j * R : (j + 1) * R]
        if layer == 0:
            lS[layer, 8:16, :] = jnp.concatenate(
                [dest_row, valid_row, jnp.zeros((6, R), F32)], axis=0
            )
        else:
            lS[layer, 8:16, :] = jnp.zeros((8, R), F32)

    sent = []

    def send_summary(layer):
        got = []
        for k in range(1, NC):
            cp = mesh_copy(
                lS.at[layer],
                lR.at[layer, c],
                l_send.at[layer, k],
                l_recv.at[layer, k],
                t,
                curve_peer[k],
            )
            cp.start()
            got.append(cp)
            cp = mesh_copy(
                sA.at[layer, curve_peer[k]],
                rA.at[layer, c],
                a_send.at[layer, k],
                a_recv.at[layer, k],
                t,
                curve_peer[k],
            )
            cp.start()
            got.append(cp)
        lR[layer, c] = lS[layer]
        rA[layer, c] = sA[layer, c]
        sent.extend(got)
        return got

    def arrive(copies):
        for cp in copies:
            cp.wait_recv()

    def chain(layer):
        logs = [lR[layer, s, pl.ds(c, 1), :] for s in range(NC)]
        if layer == 0:
            place = [jnp.full((1, R), float(s), F32) for s in range(NC)]
        else:
            place = [lR[0, s, 8:9, :] for s in range(NC)]

        def lap(p, carry):
            state, log_sum = carry
            if layer == 0:
                sC[0, p] = state.astype(BF16)
            else:
                pre[p] = state
                lpre[p] = jnp.broadcast_to(log_sum, (8, R))
            pf = p.astype(F32)
            here = [jnp.where(place[s] == pf, 1.0, 0.0) for s in range(NC)]
            log_p = here[0] * logs[0]
            new = here[0] * rA[layer, 0].astype(F32)
            for s in range(1, NC):
                log_p = log_p + here[s] * logs[s]
                new = new + here[s] * rA[layer, s].astype(F32)
            return jnp.exp(log_p) * state + new, log_sum + log_p

        return lax.fori_loop(0, NC, lap, (jnp.zeros((R, R), F32), jnp.zeros((1, R), F32)))

    def send_carried(layer):
        got = []
        for k in range(1, NC):
            cp = mesh_copy(
                sC.at[layer, curve_peer[k]],
                rC.at[layer, c],
                c_send.at[layer, k],
                c_recv.at[layer, k],
                t,
                curve_peer[k],
            )
            cp.start()
            got.append(cp)
        rC[layer, c] = sC[layer, c]
        sent.extend(got)
        return got

    def inside(layer, steps, running, keys, queries):
        scores = lax.dot_general(
            queries, keys.astype(BF16), (((1,), (1,)), ((), ())), preferred_element_type=F32
        )
        scores = jnp.where(causal, scores, 0.0)
        running_t = running.T
        steps_t = steps.T
        half = lane < 64
        decx[...] = widen(jnp.exp(running))

        for j in range(NC):
            cols = slice(j * R, (j + 1) * R)
            v = vals[:, cols]
            vf = v.astype(F32)
            acc = skip_x[layer : layer + 1, cols] * vf
            for e in range(2):
                h = 2 * j + e
                gap = running[:, h : h + 1] - running_t[h : h + 1, :]
                w = jnp.exp(jnp.minimum(gap, 0.0)) * steps_t[h : h + 1, :] * scores
                ve = jnp.where(half if e == 0 else jnp.logical_not(half), vf, 0.0)
                acc = acc + jnp.dot(w.astype(BF16), ve.astype(BF16), preferred_element_type=F32)
            inner[:, cols] = acc

    def finish(layer, xb, live_col, queries):
        squares = jnp.zeros((R, R), F32)
        for j in range(NC):
            cols = slice(j * R, (j + 1) * R)
            from_state = jnp.dot(queries, rC[layer, j], preferred_element_type=F32)
            g = (inner[:, cols] + decx[:, cols] * from_state) * gate[:, cols]
            squares = squares + g * g
            inner[:, cols] = g
        scale = lax.rsqrt(jnp.sum(squares, axis=-1, keepdims=True) * (1.0 / E) + 1e-05)
        scaled = (inner[...] * scale * gg[layer : layer + 1, :]).astype(BF16)
        update = jnp.dot(scaled, wout[layer], preferred_element_type=F32)
        return (xb.astype(F32) + live_col * update).astype(BF16)

    xb = x_v[...]
    live = jnp.where(row_f < valid_row, 1.0, 0.0)
    nb = norm_of(xb, 0)
    dt_cp[0].wait()
    steps, running = times_of(nb, live, 0)
    bc_cp[0].wait()
    keys = keys_of(nb, 0)
    xz_cp[0][0].wait()
    xz_cp[0][1].wait()
    project_values(nb, 0)
    summary(0, steps, running, keys)
    pl.semaphore_wait(barrier, (NC - 1) + (NZ - 1) + (NY - 1))
    got = send_summary(0)
    dt_cp.append(fetch(wdt_h.at[1], wdt.at[1]))
    bc_cp.append(fetch(wbc_h.at[1], wbc.at[1]))
    xz_cp.append(fetch_xz(1))
    out_cp.append(fetch(wout_h.at[1], wout.at[1]))
    xz_cp[0][2].wait()
    xz_cp[0][3].wait()
    project_gate(nb, 0)
    queries = queries_of(nb, 0)
    arrive(got)
    chain(0)
    got = send_carried(0)
    inside(0, steps, running, keys, queries)
    out_cp[0].wait()
    arrive(got)
    first = finish(0, xb, live[:, 0:1], queries)
    mS[...] = first

    nb = norm_of(first, 1)
    dt_cp[1].wait()
    steps, running = times_of(nb, live, 1)
    bc_cp[1].wait()
    keys = keys_of(nb, 1)
    for cp in xz_cp[1]:
        cp.wait()
    out_cp[1].wait()
    project_values(nb, 1)
    summary(1, steps, running, keys)
    got_a = send_summary(1)

    got_m = []
    for k in range(1, 4):
        cp = mesh_copy(
            mS, mR.at[k], m_send.at[k], m_recv.at[k], t, lax.rem(c + 2 * k, NC)
        )
        cp.start()
        got_m.append(cp)
    sent.extend(got_m)

    arrive(got_a)
    tile_state, tile_log = chain(1)
    for k in range(NZ):
        sB1[k, 0:RZ, :] = tile_state[k * RZ : (k + 1) * RZ, :]
        sB1[k, RZ : RZ + 8, :] = jnp.broadcast_to(tile_log, (8, R))
    got = []
    for k in range(1, NZ):
        cp = mesh_copy(
            sB1.at[z_peer[k]],
            rB1.at[z],
            b1_send.at[k],
            b1_recv.at[k],
            y * NZ + z_peer[k],
            c,
        )
        cp.start()
        got.append(cp)
    rB1[z] = sB1[z]
    sent.extend(got)
    arrive(got)

    state = jnp.zeros((RZ, R), F32)
    log_sum = jnp.zeros((1, R), F32)
    row_states, row_logs = [], []
    for k in range(NZ):
        row_states.append(state)
        row_logs.append(log_sum)
        log_k = rB1[k, RZ : RZ + 1, :]
        state = jnp.exp(log_k) * state + rB1[k, 0:RZ, :]
        log_sum = log_sum + log_k
    sB2[0:RZ, :] = state
    sB2[RZ : RZ + 8, :] = jnp.broadcast_to(log_sum, (8, R))
    got = []
    for k in range(1, NY):
        cp = mesh_copy(
            sB2, rB2.at[y], b2_send.at[k], b2_recv.at[k], y_peer[k] * NZ + z, c
        )
        cp.start()
        got.append(cp)
    rB2[y] = sB2[...]
    sent.extend(got)

    arrive(got_m)
    partner = c + 1 - 2 * lax.rem(c, 2)
    c_f, partner_f = c.astype(F32), partner.astype(F32)
    mine = jnp.zeros((R, D), F32)
    theirs = jnp.zeros((R, D), F32)
    for k in range(4):
        src = lax.rem(c + NC - 2 * k, NC)
        goes = lR[0, src, 8:9, :]
        blk = (first if k == 0 else mR[k]).astype(F32)
        m_mine = jnp.concatenate([jnp.where(goes == c_f, 1.0, 0.0)] * 4, axis=1)
        m_theirs = jnp.concatenate([jnp.where(goes == partner_f, 1.0, 0.0)] * 4, axis=1)
        mine = mine + m_mine * blk
        theirs = theirs + m_theirs * blk
    pS[...] = theirs.astype(BF16)
    swap = mesh_copy(pS, pR, m_send.at[0], m_recv.at[0], t, partner)
    swap.start()
    sent.append(swap)
    valid_row = jnp.zeros((1, R), F32)
    for s in range(NC):
        valid_row = valid_row + jnp.where(lR[0, s, 8:9, :] == c_f, 1.0, 0.0) * lR[0, s, 9:10, :]
    live = jnp.where(row_f < valid_row, 1.0, 0.0)

    arrive(got)
    state = jnp.zeros((RZ, R), F32)
    for k in range(NY):
        new = jnp.exp(rB2[k, RZ : RZ + 1, :]) * state + rB2[k, 0:RZ, :]
        state = jnp.where(k < y, new, state)
    for k in range(NZ):
        sB3[k] = (jnp.exp(row_logs[k]) * state + row_states[k]).astype(BF16)
    got = []
    for k in range(1, NZ):
        cp = mesh_copy(
            sB3.at[z_peer[k]],
            rB3.at[z],
            b3_send.at[k],
            b3_recv.at[k],
            y * NZ + z_peer[k],
            c,
        )
        cp.start()
        got.append(cp)
    rB3[z] = sB3[z]
    sent.extend(got)

    swap.wait_recv()
    xb = (mine + pR[...].astype(F32)).astype(BF16)
    nb = norm_of(xb, 1)
    steps, running = times_of(nb, live, 1)
    keys = keys_of(nb, 1)
    queries = queries_of(nb, 1)
    project_values(nb, 1)

    arrive(got)
    entry = jnp.concatenate([rB3[k].astype(F32) for k in range(NZ)], axis=0)
    for p in range(NC):
        sC[1, p] = (jnp.exp(lpre[p, 0:1, :]) * entry + pre[p]).astype(BF16)
    got = send_carried(1)
    project_gate(nb, 1)
    inside(1, steps, running, keys, queries)
    arrive(got)
    out_v[...] = finish(1, xb, live[:, 0:1], queries)
    done = pltpu.make_async_copy(out_v, out_h.at[0], out_sem)
    done.start()
    for cp in sent:
        cp.wait_send()
    done.wait()


def call(NY, NZ, points, valid_rows, dest_shard, *params):
    RZ = R // NZ
    V = pltpu.VMEM
    DMA = pltpu.SemaphoreType.DMA
    hbm = pl.BlockSpec(memory_space=pltpu.HBM)
    smem = pl.BlockSpec(memory_space=pltpu.SMEM)
    return pl.pallas_call(
        functools.partial(kernel, NY, NZ),
        out_shape=jax.ShapeDtypeStruct(points.shape, points.dtype),
        in_specs=[smem, smem] + [hbm] * 10,
        out_specs=hbm,
        scratch_shapes=[
            V((R, D), BF16),
            V((2, D), F32),
            V((2, 2 * E // CH, D, CH), BF16),
            V((2, D, 2 * R), BF16),
            V((2, H, D), BF16),
            V((2, H), F32),
            V((2, H), F32),
            V((2, H), F32),
            V((2, E), F32),
            V((2, E, D), BF16),
            DMA((20,)),
            V((R, E), BF16),
            V((R, E), BF16),
            V((R, E), F32),
            V((R, E), F32),
            V((R, E), F32),
            V((2, NC, R, R), BF16),
            V((2, NC, R, R), BF16),
            V((2, 16, R), F32),
            V((2, NC, 16, R), F32),
            V((2, NC, R, R), BF16),
            V((2, NC, R, R), BF16),
            V((NC, R, R), F32),
            V((NC, 8, R), F32),
            V((NZ, RZ + 8, R), F32),
            V((NZ, RZ + 8, R), F32),
            V((RZ + 8, R), F32),
            V((NY, RZ + 8, R), F32),
            V((NZ, RZ, R), BF16),
            V((NZ, RZ, R), BF16),
            V((R, D), BF16),
            V((4, R, D), BF16),
            V((R, D), BF16),
            V((R, D), BF16),
            V((R, D), BF16),
            DMA((2, NC)),
            DMA((2, NC)),
            DMA((2, NC)),
            DMA((2, NC)),
            DMA((2, NC)),
            DMA((2, NC)),
            DMA((NZ,)),
            DMA((NZ,)),
            DMA((NY,)),
            DMA((NY,)),
            DMA((NZ,)),
            DMA((NZ,)),
            DMA((4,)),
            DMA((4,)),
            DMA(()),
        ],
        compiler_params=pltpu.CompilerParams(
            collective_id=0, has_side_effects=True, vmem_limit_bytes=67043328
        ),
    )(valid_rows, dest_shard, points, *params)


def solution(mesh):
    tiles = mesh.shape["tile"]
    NZ = min(8, max(1, tiles // 2))
    NY = tiles // NZ

    def local(points, valid_rows, dest_shard, dest_slot, ng, wxz, wbc, wdt, *params):
        wdt = jnp.transpose(wdt, (0, 2, 1))
        return call(NY, NZ, points, valid_rows, dest_shard, ng, wxz, wbc, wdt, *params)

    in_specs = (
        P("tile", "curve", None),
        P("tile", "curve"),
        P("tile", "curve", None),
        P("tile", "curve", None),
    ) + (P(),) * 9
    return jax.shard_map(
        local, mesh=mesh, in_specs=in_specs, out_specs=P("tile", "curve", None), check_vma=False
    )
```

```python
import functools

import jax
import jax.numpy as jnp
from jax import lax
from jax.experimental import pallas as pl
from jax.experimental.pallas import tpu as pltpu
from jax.sharding import PartitionSpec as P

F32 = jnp.float32
BF16 = jnp.bfloat16
HI = lax.Precision.HIGHEST
NC = 8
R = 128
D = 512
E = 1024
H = 16
CH = 512


def silu(v):
    return v * jax.nn.sigmoid(v)


def softplus(v):
    return jnp.maximum(v, 0.0) + jnp.log1p(jnp.exp(-jnp.abs(v)))


def mesh_copy(src, dst, send_sem, recv_sem, tile, curve):
    return pltpu.make_async_remote_copy(
        src_ref=src,
        dst_ref=dst,
        send_sem=send_sem,
        recv_sem=recv_sem,
        device_id=(tile, curve),
        device_id_type=pl.DeviceIdType.MESH,
    )


def kernel(
    NY,
    NZ,
    valid_s,
    dest_s,
    x_h,
    ng_h,
    wxz_h,
    wbc_h,
    wdt_h,
    dtb_h,
    rate_h,
    skip_h,
    gg_h,
    wout_h,
    out_h,
    x_v,
    ng,
    wxz,
    wbc,
    wdt,
    dtb,
    rate,
    skip,
    gg,
    wout,
    in_sem,
    exp_m,
    vals,
    gate,
    inner,
    decx,
    scaled,
    sA,
    rA,
    lS,
    lR,
    iS,
    iR,
    sC,
    rC,
    pre,
    lpre,
    tS,
    tR,
    sB1,
    rB1,
    sB3,
    rB3,
    mS,
    mR,
    pS,
    pR,
    a_send,
    a_recv,
    l_send,
    l_recv,
    i_send,
    i_recv,
    c_send,
    c_recv,
    t_send,
    t_recv,
    b1_send,
    b1_recv,
    b3_send,
    b3_recv,
    m_send,
    m_recv,
    ready,
):
    t = lax.axis_index("tile")
    c = lax.axis_index("curve")
    y = t // NZ
    z = lax.rem(t, NZ)
    RZ = R // NZ
    curve_peer = [lax.rem(c + k, NC) for k in range(NC)]
    z_peer = [lax.rem(z + k, NZ) for k in range(NZ)]
    far_first = (4, 5, 3, 2, 6, 7, 1)

    n_in = [0]

    def fetch(src, dst):
        cp = pltpu.make_async_copy(src, dst, in_sem.at[n_in[0]])
        n_in[0] += 1
        cp.start()
        return cp

    def fetch_xz(layer):
        return [
            fetch(wxz_h.at[layer, :, pl.ds(q * CH, CH)], wxz.at[layer, q])
            for q in range(2 * E // CH)
        ]

    x_cp = fetch(x_h.at[0], x_v)
    dt_cp = [fetch(wdt_h.at[0], wdt.at[0])]
    small_cp = [
        fetch(a, b)
        for a, b in ((ng_h, ng), (dtb_h, dtb), (rate_h, rate), (skip_h, skip), (gg_h, gg))
    ]
    bc_cp = [fetch(wbc_h.at[0], wbc.at[0])]
    xz_cp = [fetch_xz(0)]
    out_cp = [fetch(wout_h.at[0], wout.at[0])]

    barrier = pltpu.get_barrier_semaphore()

    def signal(sem, tile, curve):
        pl.semaphore_signal(
            sem, inc=1, device_id=(tile, curve), device_id_type=pl.DeviceIdType.MESH
        )

    for k in range(1, NC):
        signal(barrier, t, curve_peer[k])
    for k in range(1, NZ):
        signal(barrier, y * NZ + z_peer[k], c)
    for a in range(1, NY):

        @pl.when(y + a < NY)
        def _():
            for k in range(NZ):
                signal(barrier, (y + a) * NZ + k, c)

    lane = lax.broadcasted_iota(jnp.int32, (R, R), 1)
    row = lax.broadcasted_iota(jnp.int32, (R, R), 0)
    row_f = row.astype(F32)
    causal = row >= lane
    tri = jnp.where(causal, 1.0, 0.0).astype(F32)
    for j in range(NC):
        exp_m[j] = jnp.where(
            jnp.logical_and(row < 48, (row & 15) == (lane >> 6) + 2 * j), 1.0, 0.0
        ).astype(BF16)
    rep = jnp.where(
        lax.broadcasted_iota(jnp.int32, (H, R), 0)
        == (lax.broadcasted_iota(jnp.int32, (H, R), 1) & 15),
        1.0,
        0.0,
    )

    def parts_of(v):
        hi = v.astype(BF16).astype(F32)
        rest = v - hi
        mid = rest.astype(BF16).astype(F32)
        low = rest - mid
        ln = lax.broadcasted_iota(jnp.int32, v.shape, 1)
        return jnp.where(ln < 16, hi, jnp.where(ln < 32, mid, low)).astype(BF16)

    def widen(parts, j):
        return jnp.dot(parts, exp_m[j], preferred_element_type=F32)

    def copies8(v):
        return jnp.dot(v, rep, precision=HI, preferred_element_type=F32)

    valid_row = jnp.full((1, R), valid_s[0, 0], jnp.int32).astype(F32)
    dest_row = jnp.full((1, R), dest_s[0, 0, 0], jnp.int32).astype(F32)
    iS[0:1, :] = dest_row
    iS[1:2, :] = valid_row

    def norm_of(xb, layer):
        w = xb.astype(F32)
        ms = jnp.mean(w * w, axis=-1, keepdims=True)
        return (w * lax.rsqrt(ms + 1e-05) * ng[layer : layer + 1, :]).astype(BF16)

    def times_of(nb, live, layer):
        wrep = jnp.concatenate([wdt[layer]] * 8, axis=0)
        raw = lax.dot_general(
            nb, wrep, (((1,), (1,)), ((), ())), preferred_element_type=F32
        )
        steps = softplus(raw + bias8[layer : layer + 1, :])
        steps = steps * live
        running = jnp.dot(
            tri, -steps * rate8[layer : layer + 1, :], precision=HI, preferred_element_type=F32
        )
        return steps, running

    def project_values(nb, layer):
        for q in range(E // CH):
            v = silu(jnp.dot(nb, wxz[layer, q], preferred_element_type=F32)).astype(BF16)
            for i in range(CH // R):
                vals[q * (CH // R) + i] = v[:, i * R : (i + 1) * R]

    def project_gate(nb, layer):
        for q in range(E // CH):
            v = silu(jnp.dot(nb, wxz[layer, q + E // CH], preferred_element_type=F32))
            for i in range(CH // R):
                gate[q * (CH // R) + i] = v[:, i * R : (i + 1) * R]

    def keys_of(nb, layer):
        return silu(jnp.dot(nb, wbc[layer, :, 0:R], preferred_element_type=F32))

    def queries_of(nb, layer):
        return silu(jnp.dot(nb, wbc[layer, :, R : 2 * R], preferred_element_type=F32)).astype(BF16)

    sent = []

    def go(copy):
        copy.start()
        sent.append(copy)
        return copy

    def arrive(copies):
        for cp in copies:
            cp.wait_recv()

    def fill_logs(layer, running):
        total = parts_of(jnp.broadcast_to(running[R - 1 : R, :], (8, R)))
        for j in range(NC):
            lS[layer, j] = widen(total, j)[0:1, :]

    def send_logs(layer):
        got = []
        for k in far_first:
            got.append(
                go(
                    mesh_copy(
                        lS.at[layer, curve_peer[k]],
                        lR.at[layer, c],
                        l_send.at[layer, k],
                        l_recv.at[layer, k],
                        t,
                        curve_peer[k],
                    )
                )
            )
        lR[layer, c] = lS[layer, c]
        return got

    def send_states(layer, steps, running, keys):
        wide = parts_of(jnp.exp(running[R - 1 : R, :] - running) * steps)
        keys_t = keys.T.astype(BF16)

        def piece(j):
            scaled = (vals[j].astype(F32) * widen(wide, j)).astype(BF16)
            return jnp.dot(keys_t, scaled, preferred_element_type=F32).astype(BF16)

        got, ready = [], None
        for k in far_first:
            j = curve_peer[k]
            sA[layer, j] = piece(j)
            if ready is not None:
                got.append(go(ready))
            ready = mesh_copy(
                sA.at[layer, j],
                rA.at[layer, c],
                a_send.at[layer, k],
                a_recv.at[layer, k],
                t,
                j,
            )
        rA[layer, c] = piece(c)
        got.append(go(ready))
        return got

    def carried_copy(layer, k):
        return mesh_copy(
            sC.at[layer, curve_peer[k]],
            rC.at[layer, c],
            c_send.at[layer, k],
            c_recv.at[layer, k],
            t,
            curve_peer[k],
        )

    def scores_of(keys, queries):
        scores = lax.dot_general(
            queries, keys.astype(BF16), (((1,), (1,)), ((), ())), preferred_element_type=F32
        )
        return jnp.where(causal, scores, 0.0)

    def inside(layer, steps_t, running, running_t, scores, which):
        half = lane < 64
        wide = parts_of(jnp.exp(running))
        for j in which:
            decx[j] = widen(wide, j)
            vf = vals[j].astype(F32)
            acc = widen(skip_parts, j)[layer : layer + 1, :] * vf
            ws, ves = [], []
            for e in range(2):
                h = 2 * j + e
                gap = running[:, h : h + 1] - running_t[h : h + 1, :]
                w = jnp.exp(jnp.minimum(gap, 0.0)) * steps_t[h : h + 1, :] * scores
                ve = jnp.where(half if e == 0 else jnp.logical_not(half), vf, 0.0)
                ws.append(w.astype(BF16))
                ves.append(ve.astype(BF16))
            inner[j] = acc + jnp.dot(
                jnp.concatenate(ws, axis=1),
                jnp.concatenate(ves, axis=0),
                preferred_element_type=F32,
            )

    def finish(layer, xb, live_col, queries):
        squares = jnp.zeros((R, R), F32)
        for j in range(NC):
            from_state = jnp.dot(queries, rC[layer, j], preferred_element_type=F32)
            g = (inner[j] + decx[j] * from_state) * gate[j]
            squares = squares + g * g
            cols = slice(j * R, (j + 1) * R)
            scaled[:, cols] = (g * gg[layer : layer + 1, cols]).astype(BF16)
        scale = lax.rsqrt(jnp.sum(squares, axis=-1, keepdims=True) * (1.0 / E) + 1e-05)
        update = jnp.dot(scaled[...], wout[layer], preferred_element_type=F32)
        return (xb.astype(F32) + (live_col * scale) * update).astype(BF16)

    live = jnp.where(row_f < valid_row, 1.0, 0.0)
    x_cp.wait()
    for cp in small_cp:
        cp.wait()
    for cp in (dt_cp[0], bc_cp[0], xz_cp[0][0], xz_cp[0][1]):
        cp.wait()
    bias8, rate8 = copies8(dtb[...]), copies8(rate[...])
    skip_parts = parts_of(jnp.concatenate([copies8(skip[...])] * 4, axis=0))
    xb = x_v[...]
    nb = norm_of(xb, 0)
    steps, running = times_of(nb, live, 0)
    keys = keys_of(nb, 0)
    project_values(nb, 0)
    fill_logs(0, running)
    pl.semaphore_wait(barrier, (NC - 1) + (NZ - 1) + NZ * y)
    got_l = send_logs(0)
    got = send_states(0, steps, running, keys)
    got_i = []
    for k in far_first:
        got_i.append(
            go(mesh_copy(iS, iR.at[c], i_send.at[k], i_recv.at[k], t, curve_peer[k]))
        )
    iR[c] = iS[...]
    for a in range(1, NY):

        @pl.when(y >= a)
        def _():
            for k in range(NZ):
                signal(ready, (y - a) * NZ + k, c)

    dt_cp.append(fetch(wdt_h.at[1], wdt.at[1]))
    bc_cp.append(fetch(wbc_h.at[1], wbc.at[1]))
    xz_cp.append(fetch_xz(1))
    out_cp.append(fetch(wout_h.at[1], wout.at[1]))
    xz_cp[0][2].wait()
    xz_cp[0][3].wait()
    project_gate(nb, 0)
    queries = queries_of(nb, 0)
    scores = scores_of(keys, queries)
    running_t, steps_t = running.T, steps.T
    arrive(got_l)
    arrive(got)
    state = jnp.zeros((R, R), F32)
    for p in range(NC):
        sC[0, p] = state.astype(BF16)
        if p < NC - 1:
            state = jnp.exp(lR[0, p]) * state + rA[0, p].astype(F32)
    got = [go(carried_copy(0, k)) for k in far_first]
    rC[0, c] = sC[0, c]
    inside(0, steps_t, running, running_t, scores, range(NC))
    out_cp[0].wait()
    dt_cp[1].wait()
    bc_cp[1].wait()
    for cp in xz_cp[1]:
        cp.wait()
    out_cp[1].wait()
    arrive(got_i)
    arrive(got)
    first = finish(0, xb, live[:, 0:1], queries)
    mS[...] = first

    nb = norm_of(first, 1)
    steps, running = times_of(nb, live, 1)
    keys = keys_of(nb, 1)
    project_values(nb, 1)
    fill_logs(1, running)
    got_l = send_logs(1)
    got_a = send_states(1, steps, running, keys)

    got_m = []
    for k in (2, 1, 3):
        got_m.append(
            go(mesh_copy(mS, mR.at[k], m_send.at[k], m_recv.at[k], t, curve_peer[2 * k]))
        )

    def row_sends(start_copy):
        own = [start_copy(0, k) for k in range(1, NZ)]
        for cp in own:
            cp.start()
        later = []
        for a in range(1, NY):
            cps = [start_copy(a, k) for k in range(NZ)]

            @pl.when(y + a < NY)
            def _():
                for cp in cps:
                    cp.start()

            later.append(cps)
        return own, later

    def row_arrive(pair):
        own, later = pair
        arrive(own)
        for a in range(1, NY):

            @pl.when(y >= a)
            def _():
                arrive(later[a - 1])

    def row_sent(pair):
        own, later = pair
        for cp in own:
            cp.wait_send()
        for a in range(1, NY):

            @pl.when(y + a < NY)
            def _():
                for cp in later[a - 1]:
                    cp.wait_send()

    arrive(got_l)
    logs = [lR[1, s] for s in range(NC)]
    place = [iR[s, 0:1, :] for s in range(NC)]
    tile_log = logs[0]
    for s in range(1, NC):
        tile_log = tile_log + logs[s]
    tS[...] = tile_log
    weights = []
    for s in range(NC):
        after = jnp.zeros((1, R), F32)
        for o in range(NC):
            if o != s:
                after = after + jnp.where(place[o] > place[s], logs[o], 0.0)
        weights.append(jnp.exp(after))
    tR[y, z] = tile_log

    @pl.when(y < NY - 1)
    def _():
        pl.semaphore_wait(ready, NZ * (NY - 1 - y))

    logs_sent = row_sends(
        lambda a, k: mesh_copy(
            tS,
            tR.at[y, z],
            t_send.at[a, k],
            t_recv.at[a, k],
            (y + a) * NZ + z_peer[k],
            c,
        )
    )
    arrive(got_a)
    total = weights[0] * rA[1, 0].astype(F32)
    for s in range(1, NC):
        total = total + weights[s] * rA[1, s].astype(F32)
    for k in range(NZ):
        sB1[k] = total[k * RZ : (k + 1) * RZ, :].astype(BF16)
    rB1[y, z] = sB1[z]
    states_sent = row_sends(
        lambda a, k: mesh_copy(
            sB1.at[z_peer[k]],
            rB1.at[y, z],
            b1_send.at[a, k],
            b1_recv.at[a, k],
            (y + a) * NZ + z_peer[k],
            c,
        )
    )

    def lap(p, carry):
        state, log_sum = carry
        pre[p] = state
        lpre[p] = log_sum
        pf = p.astype(F32)
        here = [jnp.where(place[s] == pf, 1.0, 0.0) for s in range(NC)]
        log_p = here[0] * logs[0]
        new = here[0] * rA[1, 0].astype(F32)
        for s in range(1, NC):
            log_p = log_p + here[s] * logs[s]
            new = new + here[s] * rA[1, s].astype(F32)
        return jnp.exp(log_p) * state + new, log_sum + log_p

    lax.fori_loop(0, NC, lap, (jnp.zeros((R, R), F32), jnp.zeros((1, R), F32)))

    row_arrive(logs_sent)
    row_arrive(states_sent)
    state = jnp.zeros((RZ, R), F32)
    for a in range(NY - 1):
        new = state
        for k in range(NZ):
            new = jnp.exp(tR[a, k]) * new + rB1[a, k].astype(F32)
        state = jnp.where(a < y, new, state)
    for k in range(NZ):
        sB3[k] = state.astype(BF16)
        if k < NZ - 1:
            state = jnp.exp(tR[y, k]) * state + rB1[y, k].astype(F32)
    rB3[z] = sB3[z]
    got = []
    for k in (4, 3, 5, 2, 6, 1, 7) if NZ == 8 else range(1, NZ):
        got.append(
            go(
                mesh_copy(
                    sB3.at[z_peer[k]],
                    rB3.at[z],
                    b3_send.at[k],
                    b3_recv.at[k],
                    y * NZ + z_peer[k],
                    c,
                )
            )
        )
    arrive(got_m)
    partner = c + 1 - 2 * lax.rem(c, 2)
    c_f, partner_f = c.astype(F32), partner.astype(F32)
    mine = jnp.zeros((R, D), F32)
    theirs = jnp.zeros((R, D), F32)
    for k in range(4):
        goes = iR[lax.rem(c + NC - 2 * k, NC), 0:1, :]
        blk = (mS[...] if k == 0 else mR[k]).astype(F32)
        m_mine = jnp.concatenate([jnp.where(goes == c_f, 1.0, 0.0)] * 4, axis=1)
        m_theirs = jnp.concatenate([jnp.where(goes == partner_f, 1.0, 0.0)] * 4, axis=1)
        mine = mine + m_mine * blk
        theirs = theirs + m_theirs * blk
    pS[...] = theirs.astype(BF16)
    x_v[...] = mine.astype(BF16)
    valid_row = jnp.zeros((1, R), F32)
    for s in range(NC):
        valid_row = valid_row + jnp.where(place[s] == c_f, 1.0, 0.0) * iR[s, 1:2, :]
    live = jnp.where(row_f < valid_row, 1.0, 0.0)
    swap = go(mesh_copy(pS, pR, m_send.at[0], m_recv.at[0], t, partner))

    swap.wait_recv()
    xb = (x_v[...].astype(F32) + pR[...].astype(F32)).astype(BF16)
    nb = norm_of(xb, 1)
    steps, running = times_of(nb, live, 1)
    keys = keys_of(nb, 1)
    queries = queries_of(nb, 1)
    project_values(nb, 1)

    project_gate(nb, 1)
    scores = scores_of(keys, queries)
    running_t, steps_t = running.T, steps.T
    arrive(got)
    entry = jnp.concatenate([rB3[k].astype(F32) for k in range(NZ)], axis=0)
    got, ready = [], None
    for k in far_first:
        p = curve_peer[k]
        sC[1, p] = (jnp.exp(lpre[p]) * entry + pre[p]).astype(BF16)
        if ready is not None:
            got.append(go(ready))
        ready = carried_copy(1, k)
    rC[1, c] = (jnp.exp(lpre[c]) * entry + pre[c]).astype(BF16)
    got.append(go(ready))
    inside(1, steps_t, running, running_t, scores, range(NC))
    last = {id(cp) for cp in got}
    for cp in sent:
        if id(cp) not in last:
            cp.wait_send()
    row_sent(logs_sent)
    row_sent(states_sent)
    arrive(got)
    out_h[0] = finish(1, xb, live[:, 0:1], queries)
    for cp in got:
        cp.wait_send()


def call(NY, NZ, points, valid_rows, dest_shard, *params):
    RZ = R // NZ
    V = pltpu.VMEM
    DMA = pltpu.SemaphoreType.DMA
    hbm = pl.BlockSpec(memory_space=pltpu.HBM)
    smem = pl.BlockSpec(memory_space=pltpu.SMEM)
    return pl.pallas_call(
        functools.partial(kernel, NY, NZ),
        out_shape=jax.ShapeDtypeStruct(points.shape, points.dtype),
        in_specs=[smem, smem] + [hbm] * 10,
        out_specs=pl.BlockSpec(memory_space=pltpu.VMEM),
        scratch_shapes=[
            V((R, D), BF16),
            V((2, D), F32),
            V((2, 2 * E // CH, D, CH), BF16),
            V((2, D, 2 * R), BF16),
            V((2, H, D), BF16),
            V((2, H), F32),
            V((2, H), F32),
            V((2, H), F32),
            V((2, E), F32),
            V((2, E, D), BF16),
            DMA((20,)),
            V((NC, R, R), BF16),
            V((NC, R, R), BF16),
            V((NC, R, R), F32),
            V((NC, R, R), F32),
            V((NC, R, R), F32),
            V((R, E), BF16),
            V((2, NC, R, R), BF16),
            V((2, NC, R, R), BF16),
            V((2, NC, 1, R), F32),
            V((2, NC, 1, R), F32),
            V((2, R), F32),
            V((NC, 2, R), F32),
            V((2, NC, R, R), BF16),
            V((2, NC, R, R), BF16),
            V((NC, R, R), F32),
            V((NC, 1, R), F32),
            V((1, R), F32),
            V((NY, NZ, 1, R), F32),
            V((NZ, RZ, R), BF16),
            V((NY, NZ, RZ, R), BF16),
            V((NZ, RZ, R), BF16),
            V((NZ, RZ, R), BF16),
            V((R, D), BF16),
            V((4, R, D), BF16),
            V((R, D), BF16),
            V((R, D), BF16),
            DMA((2, NC)),
            DMA((2, NC)),
            DMA((2, NC)),
            DMA((2, NC)),
            DMA((NC,)),
            DMA((NC,)),
            DMA((2, NC)),
            DMA((2, NC)),
            DMA((NY, NZ)),
            DMA((NY, NZ)),
            DMA((NY, NZ)),
            DMA((NY, NZ)),
            DMA((NZ,)),
            DMA((NZ,)),
            DMA((4,)),
            DMA((4,)),
            pltpu.SemaphoreType.REGULAR,
        ],
        compiler_params=pltpu.CompilerParams(
            collective_id=0, has_side_effects=True, vmem_limit_bytes=40 * 1024 * 1024
        ),
    )(valid_rows, dest_shard, *[pltpu.with_memory_space_constraint(v, pltpu.HBM) for v in (points, *params)])


def solution(mesh):
    tiles = mesh.shape["tile"]
    NZ = min(8, max(1, tiles // 2))
    NY = tiles // NZ

    def local(points, valid_rows, dest_shard, dest_slot, ng, wxz, wbc, wdt, *params):
        wdt = jnp.transpose(wdt, (0, 2, 1))
        return call(NY, NZ, points, valid_rows, dest_shard, ng, wxz, wbc, wdt, *params)

    in_specs = (
        P("tile", "curve", None),
        P("tile", "curve"),
        P("tile", "curve", None),
        P("tile", "curve", None),
    ) + (P(),) * 9
    return jax.shard_map(
        local, mesh=mesh, in_specs=in_specs, out_specs=P("tile", "curve", None), check_vma=False
    )
```

```python
import functools

import jax
import jax.numpy as jnp
from jax import lax
from jax.experimental import pallas as pl
from jax.experimental.pallas import tpu as pltpu
from jax.sharding import PartitionSpec as P

F32 = jnp.float32
BF16 = jnp.bfloat16
HI = lax.Precision.HIGHEST
NC = 8
R = 128
D = 512
E = 1024
H = 16
CH = 512
W = 256
NX = E // W


def silu(v):
    return v * jax.nn.sigmoid(v)


def softplus(v):
    return jnp.maximum(v, 0.0) + jnp.log1p(jnp.exp(-jnp.abs(v)))


def mesh_copy(src, dst, send_sem, recv_sem, tile, curve):
    return pltpu.make_async_remote_copy(
        src_ref=src,
        dst_ref=dst,
        send_sem=send_sem,
        recv_sem=recv_sem,
        device_id=(tile, curve),
        device_id_type=pl.DeviceIdType.MESH,
    )


def kernel(
    NY,
    NZ,
    valid_v,
    dest_v,
    x_h,
    ng_h,
    wxz_h,
    wbc_h,
    wdt_h,
    dtb_h,
    rate_h,
    skip_h,
    gg_h,
    wout_h,
    out_h,
    x_v,
    ng,
    wxz,
    wbc,
    wdt,
    dtb,
    rate,
    skip,
    gg,
    wout,
    in_sem,
    exp_m,
    vals,
    gate,
    inner,
    decx,
    acc,
    ggx,
    sA,
    rA,
    lS,
    lR,
    iS,
    iR,
    sC,
    rC,
    pre,
    lpre,
    tS,
    tR,
    sB1,
    rB1,
    sB3,
    rB3,
    mS,
    mR,
    pS,
    pR,
    a_send,
    a_recv,
    l_send,
    l_recv,
    i_send,
    i_recv,
    c_send,
    c_recv,
    t_send,
    t_recv,
    b1_send,
    b1_recv,
    b3_send,
    b3_recv,
    m_send,
    m_recv,
    ready,
):
    t = lax.axis_index("tile")
    c = lax.axis_index("curve")
    y = t // NZ
    z = lax.rem(t, NZ)
    RZ = R // NZ
    curve_peer = [lax.rem(c + k, NC) for k in range(NC)]
    z_peer = [lax.rem(z + k, NZ) for k in range(NZ)]
    x = c // 2
    partner = c + 1 - 2 * lax.rem(c, 2)
    far_first = (4, 5, 3, 2, 6, 7, 1)

    barrier = pltpu.get_barrier_semaphore()

    def signal(sem, tile, curve):
        pl.semaphore_signal(
            sem, inc=1, device_id=(tile, curve), device_id_type=pl.DeviceIdType.MESH
        )

    def each_tile(first, last, sem):
        def one(i, _):
            signal(sem, i, c)
            return 0

        lax.fori_loop(first, last, one, 0)

    for k in range(1, NC):
        signal(barrier, t, curve_peer[k])
    each_tile(t + 1, NY * NZ, barrier)

    n_in = [0]

    def fetch(src, dst):
        cp = pltpu.make_async_copy(src, dst, in_sem.at[n_in[0]])
        n_in[0] += 1
        cp.start()
        return cp

    def fetch_xz(layer):
        return [
            fetch(wxz_h.at[layer, :, pl.ds(q * CH, CH)], wxz.at[layer, q])
            for q in range(2 * E // CH)
        ]

    small_cp = [fetch(a, b) for a, b in ((dtb_h, dtb), (rate_h, rate), (skip_h, skip))]
    x_cp = fetch(x_h.at[0], x_v)
    small_cp += [fetch(ng_h, ng)]
    dt_cp = [fetch(wdt_h.at[0], wdt.at[0])]
    xz_cp = [fetch_xz(0)]
    bc_cp = [fetch(wbc_h.at[0], wbc.at[0])]
    small_cp += [fetch(gg_h, gg)]
    out_cp = [fetch(wout_h.at[0], wout.at[0])]

    lane = lax.broadcasted_iota(jnp.int32, (R, R), 1)
    row = lax.broadcasted_iota(jnp.int32, (R, R), 0)
    row_f = row.astype(F32)
    causal = row >= lane
    tri = jnp.concatenate([jnp.where(causal, 1.0, 0.0).astype(BF16)] * 3, axis=1)
    for j in range(NC):
        exp_m[j // 2, :, (j % 2) * R : (j % 2 + 1) * R] = jnp.where(
            jnp.logical_and(row < 48, (row & 15) == (lane >> 6) + 2 * j), 1.0, 0.0
        ).astype(BF16)
    rep = jnp.where(
        lax.broadcasted_iota(jnp.int32, (H, R), 0)
        == (lax.broadcasted_iota(jnp.int32, (H, R), 1) & 15),
        1.0,
        0.0,
    )

    def parts_of(v):
        hi = v.astype(BF16).astype(F32)
        rest = v - hi
        mid = rest.astype(BF16).astype(F32)
        low = rest - mid
        ln = lax.broadcasted_iota(jnp.int32, v.shape, 1)
        return jnp.where(ln < 16, hi, jnp.where(ln < 32, mid, low)).astype(BF16)

    def widen(parts, q):
        return jnp.dot(parts, exp_m[q], preferred_element_type=F32)

    def copies8(v):
        return jnp.dot(v, rep, precision=HI, preferred_element_type=F32)


    def norm_of(xb, layer):
        w = xb.astype(F32)
        ms = jnp.mean(w * w, axis=-1, keepdims=True)
        return (w * lax.rsqrt(ms + 1e-05) * ng[layer : layer + 1, :]).astype(BF16)

    def times_of(nb, live, layer):
        wrep = jnp.concatenate([wdt[layer]] * 8, axis=0)
        raw = lax.dot_general(
            nb, wrep, (((1,), (1,)), ((), ())), preferred_element_type=F32
        )
        steps = softplus(raw + bias8[layer : layer + 1, :])
        steps = steps * live
        fall = -steps * rate8[layer : layer + 1, :]
        hi = fall.astype(BF16)
        rest = fall - hi.astype(F32)
        mid = rest.astype(BF16)
        low = (rest - mid.astype(F32)).astype(BF16)
        running = jnp.dot(
            tri, jnp.concatenate([hi, mid, low], axis=0), preferred_element_type=F32
        )
        return steps, running

    def project_values(nb, layer):
        for q in range(E // CH):
            v = silu(jnp.dot(nb, wxz[layer, q], preferred_element_type=F32)).astype(BF16)
            for i in range(CH // W):
                vals[q * (CH // W) + i] = v[:, i * W : (i + 1) * W]

    def project_gate(nb, layer):
        for q in range(E // CH):
            v = silu(jnp.dot(nb, wxz[layer, q + E // CH], preferred_element_type=F32))
            for i in range(CH // W):
                gate[q * (CH // W) + i] = v[:, i * W : (i + 1) * W]

    def keys_of(nb, layer):
        return silu(jnp.dot(nb, wbc[layer, :, 0:R], preferred_element_type=F32))

    def queries_of(nb, layer):
        return silu(jnp.dot(nb, wbc[layer, :, R : 2 * R], preferred_element_type=F32)).astype(BF16)

    sent = []

    def go(copy):
        copy.start()
        sent.append(copy)
        return copy

    def arrive(copies):
        for cp in copies:
            cp.wait_recv()

    def fill_logs(layer, running):
        total = parts_of(jnp.broadcast_to(running[R - 1 : R, :], (8, R)))
        for q in range(NX):
            wide = widen(total, q)
            lS[layer, 2 * q] = wide[0:1, :R]
            lS[layer, 2 * q + 1] = wide[0:1, R:]

    def send_logs(layer):
        got = []
        for k in far_first:
            got.append(
                go(
                    mesh_copy(
                        lS.at[layer, curve_peer[k]],
                        lR.at[layer, c],
                        l_send.at[layer, k],
                        l_recv.at[layer, k],
                        t,
                        curve_peer[k],
                    )
                )
            )
        lR[layer, c] = lS[layer, c]
        return got

    def make_states(layer, steps, running, keys):
        wide = parts_of(jnp.exp(running[R - 1 : R, :] - running) * steps)
        keys_t = keys.T.astype(BF16)

        for q in range(NX):
            scaled = (vals[q].astype(F32) * widen(wide, q)).astype(BF16)
            both = jnp.dot(keys_t, scaled, preferred_element_type=F32).astype(BF16)
            sA[layer, 2 * q] = both[:, :R]
            sA[layer, 2 * q + 1] = both[:, R:]

    def send_states(layer):
        got_l, got = send_logs(layer), []

        def send(j):
            k = lax.rem(j - c + NC, NC)
            got.append(
                go(
                    mesh_copy(
                        sA.at[layer, j],
                        rA.at[layer, c],
                        a_send.at[layer, k],
                        a_recv.at[layer, k],
                        t,
                        j,
                    )
                )
            )

        chip = [lax.rem(x + d, NX) for d in range(NX)]
        for d in (2, 1, 3):
            send(2 * chip[d])
            send(2 * chip[d] + 1)
        send(partner)
        rA[layer, c] = sA[layer, c]
        return got_l, got

    def carried_copy(layer, k):
        return mesh_copy(
            sC.at[layer, curve_peer[k]],
            rC.at[layer, c],
            c_send.at[layer, k],
            c_recv.at[layer, k],
            t,
            curve_peer[k],
        )

    def scores_of(keys, queries):
        scores = lax.dot_general(
            queries, keys.astype(BF16), (((1,), (1,)), ((), ())), preferred_element_type=F32
        )
        return jnp.where(causal, scores, 0.0)

    def inside(layer, steps_t, running, running_t, scores, which):
        half = lane < 64
        wide = parts_of(jnp.exp(running))
        for q in which:
            decx[q] = widen(wide, q)
            skips = widen(skip_parts, q)[layer : layer + 1, :]
            for j in (2 * q, 2 * q + 1):
                cols = slice((j % 2) * R, (j % 2 + 1) * R)
                vf = vals[q, :, cols].astype(F32)
                ws, ves = [], []
                for e in range(2):
                    h = 2 * j + e
                    gap = running[:, h : h + 1] - running_t[h : h + 1, :]
                    w = jnp.exp(jnp.minimum(gap, 0.0)) * steps_t[h : h + 1, :] * scores
                    ve = jnp.where(half if e == 0 else jnp.logical_not(half), vf, 0.0)
                    ws.append(w.astype(BF16))
                    ves.append(ve.astype(BF16))
                inner[q, :, cols] = skips[:, cols] * vf + jnp.dot(
                    jnp.concatenate(ws, axis=1),
                    jnp.concatenate(ves, axis=0),
                    preferred_element_type=F32,
                )

    def finish(layer, xb, live_col, queries):
        squares = jnp.zeros((R, W), F32)
        for d in (0, 1, 3, 2):
            xs = lax.rem(x + 4 - d, 4)
            both = (2 * xs, 2 * xs + 1)
            for src in (partner,) if d == 0 else both:
                mesh_copy(
                    sC.at[layer, src],
                    rC.at[layer, src],
                    c_send.at[layer, 0],
                    c_recv.at[layer, lax.rem(c - src + NC, NC)],
                    t,
                    src,
                ).wait_recv()
            states = jnp.concatenate([rC[layer, both[0]], rC[layer, both[1]]], axis=1)
            from_state = jnp.dot(queries, states, preferred_element_type=F32)
            g = (inner[xs] + decx[xs] * from_state) * gate[xs]
            squares = squares + g * g
            block = (g * ggx[layer, xs]).astype(BF16)
            rows = pl.ds(pl.multiple_of(xs * (2 * R), 2 * R), 2 * R)
            new = jnp.dot(block, wout[layer, rows, :], preferred_element_type=F32)
            if d == 0:
                acc[...] = new
            elif d != 2:
                acc[...] += new
        scale = lax.rsqrt(jnp.sum(squares, axis=-1, keepdims=True) * (1.0 / E) + 1e-05)
        update = acc[...] + new
        return (xb.astype(F32) + (live_col * scale) * update).astype(BF16)

    for cp in small_cp[:3]:
        cp.wait()
    valid_row = jnp.broadcast_to(valid_v[...], (1, R)).astype(F32)
    iS[0:1, :] = jnp.broadcast_to(dest_v[...], (1, R)).astype(F32)
    iS[1:2, :] = valid_row
    live = jnp.where(row_f < valid_row, 1.0, 0.0)
    bias8, rate8 = copies8(dtb[...]), copies8(rate[...])
    skip_parts = parts_of(jnp.concatenate([copies8(skip[...])] * 4, axis=0))
    x_cp.wait()
    small_cp[3].wait()
    xb = x_v[...]
    nb = norm_of(xb, 0)
    for cp in (dt_cp[0], bc_cp[0], xz_cp[0][0], xz_cp[0][1]):
        cp.wait()
    steps, running = times_of(nb, live, 0)
    keys = keys_of(nb, 0)
    project_values(nb, 0)
    fill_logs(0, running)
    make_states(0, steps, running, keys)
    pl.semaphore_wait(barrier, (NC - 1) + t)
    got_l, got = send_states(0)
    got_i = []
    for k in far_first:
        got_i.append(
            go(mesh_copy(iS, iR.at[c], i_send.at[k], i_recv.at[k], t, curve_peer[k]))
        )
    iR[c] = iS[...]
    each_tile(0, t, ready)
    small_cp[4].wait()
    for layer in range(2):
        for q in range(NX):
            ggx[layer, q] = gg[layer : layer + 1, q * W : (q + 1) * W]
    dt_cp.append(fetch(wdt_h.at[1], wdt.at[1]))
    bc_cp.append(fetch(wbc_h.at[1], wbc.at[1]))
    xz_cp.append(fetch_xz(1))
    out_cp.append(fetch(wout_h.at[1], wout.at[1]))
    xz_cp[0][2].wait()
    xz_cp[0][3].wait()
    project_gate(nb, 0)
    queries = queries_of(nb, 0)
    scores = scores_of(keys, queries)
    running_t, steps_t = running.T, steps.T
    arrive(got_l)
    arrive(got)
    state = jnp.zeros((R, R), F32)
    for p in range(NC):
        sC[0, p] = state.astype(BF16)
        if p < NC - 1:
            state = jnp.exp(lR[0, p]) * state + rA[0, p].astype(F32)
    got = [go(carried_copy(0, k)) for k in far_first]
    rC[0, c] = sC[0, c]
    inside(0, steps_t, running, running_t, scores, range(NX))
    out_cp[0].wait()
    dt_cp[1].wait()
    bc_cp[1].wait()
    for cp in xz_cp[1]:
        cp.wait()
    out_cp[1].wait()
    arrive(got_i)
    first = finish(0, xb, live[:, 0:1], queries)
    mS[...] = first

    nb = norm_of(first, 1)
    steps, running = times_of(nb, live, 1)
    keys = keys_of(nb, 1)
    project_values(nb, 1)
    fill_logs(1, running)
    make_states(1, steps, running, keys)
    got_l, got_a = send_states(1)

    got_m = []
    for k in (2, 1, 3):
        got_m.append(
            go(mesh_copy(mS, mR.at[k], m_send.at[k], m_recv.at[k], t, curve_peer[2 * k]))
        )

    far_z = (4, 3, 5, 2, 6, 1, 7, 0) if NZ == 8 else tuple(range(NZ))

    def row_sends(start_copy):
        own = [start_copy(0, k) for k in far_z if k > 0]
        later = [[start_copy(a, k) for k in far_z] for a in range(1, NY)]
        for a in (2, 1, 3) if NY == 4 else range(1, NY):
            cps = later[a - 1]

            @pl.when(y + a < NY)
            def _():
                for cp in cps:
                    cp.start()

        for cp in own:
            cp.start()
        return own, later

    def row_arrive(pair):
        own, later = pair
        arrive(own)
        for a in range(1, NY):

            @pl.when(y >= a)
            def _():
                arrive(later[a - 1])

    def row_sent(pair):
        own, later = pair
        for cp in own:
            cp.wait_send()
        for a in range(1, NY):

            @pl.when(y + a < NY)
            def _():
                for cp in later[a - 1]:
                    cp.wait_send()

    arrive(got_l)
    logs = [lR[1, s] for s in range(NC)]
    place = [iR[s, 0:1, :] for s in range(NC)]
    tile_log = logs[0]
    for s in range(1, NC):
        tile_log = tile_log + logs[s]
    tS[...] = tile_log
    weights = []
    for s in range(NC):
        after = jnp.zeros((1, R), F32)
        for o in range(NC):
            if o != s:
                after = after + jnp.where(place[o] > place[s], logs[o], 0.0)
        weights.append(jnp.exp(after))
    tR[y, z] = tile_log

    @pl.when(t < NY * NZ - 1)
    def _():
        pl.semaphore_wait(ready, NY * NZ - 1 - t)

    logs_sent = row_sends(
        lambda a, k: mesh_copy(
            tS,
            tR.at[y, z],
            t_send.at[a, k],
            t_recv.at[a, k],
            (y + a) * NZ + z_peer[k],
            c,
        )
    )
    arrive(got_a)
    total = weights[0] * rA[1, 0].astype(F32)
    for s in range(1, NC):
        total = total + weights[s] * rA[1, s].astype(F32)
    for k in range(NZ):
        sB1[k] = total[k * RZ : (k + 1) * RZ, :].astype(BF16)
    rB1[y, z] = sB1[z]
    states_sent = row_sends(
        lambda a, k: mesh_copy(
            sB1.at[z_peer[k]],
            rB1.at[y, z],
            b1_send.at[a, k],
            b1_recv.at[a, k],
            (y + a) * NZ + z_peer[k],
            c,
        )
    )

    def lap(p, carry):
        state, log_sum = carry
        pre[p] = state
        lpre[p] = log_sum
        pf = p.astype(F32)
        here = [jnp.where(place[s] == pf, 1.0, 0.0) for s in range(NC)]
        log_p = here[0] * logs[0]
        new = here[0] * rA[1, 0].astype(F32)
        for s in range(1, NC):
            log_p = log_p + here[s] * logs[s]
            new = new + here[s] * rA[1, s].astype(F32)
        return jnp.exp(log_p) * state + new, log_sum + log_p

    lax.fori_loop(0, NC, lap, (jnp.zeros((R, R), F32), jnp.zeros((1, R), F32)))

    row_arrive(logs_sent)
    row_arrive(states_sent)
    state = jnp.zeros((RZ, R), F32)
    for a in range(NY - 1):
        new = state
        for k in range(NZ):
            new = jnp.exp(tR[a, k]) * new + rB1[a, k].astype(F32)
        state = jnp.where(a < y, new, state)
    for k in range(NZ):
        sB3[k] = state.astype(BF16)
        if k < NZ - 1:
            state = jnp.exp(tR[y, k]) * state + rB1[y, k].astype(F32)
    rB3[z] = sB3[z]
    got = []
    for k in [k for k in far_z if k > 0]:
        got.append(
            go(
                mesh_copy(
                    sB3.at[z_peer[k]],
                    rB3.at[z],
                    b3_send.at[k],
                    b3_recv.at[k],
                    y * NZ + z_peer[k],
                    c,
                )
            )
        )
    arrive(got_m)
    c_f, partner_f = c.astype(F32), partner.astype(F32)
    mine = jnp.zeros((R, D), F32)
    theirs = jnp.zeros((R, D), F32)
    for k in range(4):
        goes = iR[lax.rem(c + NC - 2 * k, NC), 0:1, :]
        blk = (mS[...] if k == 0 else mR[k]).astype(F32)
        m_mine = jnp.concatenate([jnp.where(goes == c_f, 1.0, 0.0)] * 4, axis=1)
        m_theirs = jnp.concatenate([jnp.where(goes == partner_f, 1.0, 0.0)] * 4, axis=1)
        mine = mine + m_mine * blk
        theirs = theirs + m_theirs * blk
    pS[...] = theirs.astype(BF16)
    x_v[...] = mine.astype(BF16)
    valid_row = jnp.zeros((1, R), F32)
    for s in range(NC):
        valid_row = valid_row + jnp.where(place[s] == c_f, 1.0, 0.0) * iR[s, 1:2, :]
    live = jnp.where(row_f < valid_row, 1.0, 0.0)
    swap = go(mesh_copy(pS, pR, m_send.at[0], m_recv.at[0], t, partner))

    swap.wait_recv()
    xb = (x_v[...].astype(F32) + pR[...].astype(F32)).astype(BF16)
    nb = norm_of(xb, 1)
    steps, running = times_of(nb, live, 1)
    keys = keys_of(nb, 1)
    queries = queries_of(nb, 1)
    project_values(nb, 1)

    project_gate(nb, 1)
    scores = scores_of(keys, queries)
    running_t, steps_t = running.T, steps.T
    arrive(got)
    entry = jnp.concatenate([rB3[k].astype(F32) for k in range(NZ)], axis=0)
    got, ready = [], None
    for k in far_first:
        p = curve_peer[k]
        sC[1, p] = (jnp.exp(lpre[p]) * entry + pre[p]).astype(BF16)
        if ready is not None:
            got.append(go(ready))
        ready = carried_copy(1, k)
    rC[1, c] = (jnp.exp(lpre[c]) * entry + pre[c]).astype(BF16)
    got.append(go(ready))
    inside(1, steps_t, running, running_t, scores, range(NX))
    last = {id(cp) for cp in got}
    for cp in sent:
        if id(cp) not in last:
            cp.wait_send()
    row_sent(logs_sent)
    row_sent(states_sent)
    out_h[0] = finish(1, xb, live[:, 0:1], queries)
    for cp in got:
        cp.wait_send()


def call(NY, NZ, points, valid_rows, dest_shard, *params):
    RZ = R // NZ
    operands = (points, *params)
    V = pltpu.VMEM
    DMA = pltpu.SemaphoreType.DMA
    hbm = pl.BlockSpec(memory_space=pltpu.HBM)
    vmem = pl.BlockSpec(memory_space=pltpu.VMEM)
    return pl.pallas_call(
        functools.partial(kernel, NY, NZ),
        out_shape=jax.ShapeDtypeStruct(points.shape, points.dtype),
        in_specs=[vmem, vmem] + [hbm] * 10,
        out_specs=pl.BlockSpec(memory_space=pltpu.VMEM),
        scratch_shapes=[
            V((R, D), BF16),
            V((2, D), F32),
            V((2, 2 * E // CH, D, CH), BF16),
            V((2, D, 2 * R), BF16),
            V((2, H, D), BF16),
            V((2, H), F32),
            V((2, H), F32),
            V((2, H), F32),
            V((2, E), F32),
            V((2, E, D), BF16),
            DMA((20,)),
            V((NX, R, W), BF16),
            V((NX, R, W), BF16),
            V((NX, R, W), F32),
            V((NX, R, W), F32),
            V((NX, R, W), F32),
            V((R, D), F32),
            V((2, NX, 1, W), F32),
            V((2, NC, R, R), BF16),
            V((2, NC, R, R), BF16),
            V((2, NC, 1, R), F32),
            V((2, NC, 1, R), F32),
            V((2, R), F32),
            V((NC, 2, R), F32),
            V((2, NC, R, R), BF16),
            V((2, NC, R, R), BF16),
            V((NC, R, R), F32),
            V((NC, 1, R), F32),
            V((1, R), F32),
            V((NY, NZ, 1, R), F32),
            V((NZ, RZ, R), BF16),
            V((NY, NZ, RZ, R), BF16),
            V((NZ, RZ, R), BF16),
            V((NZ, RZ, R), BF16),
            V((R, D), BF16),
            V((4, R, D), BF16),
            V((R, D), BF16),
            V((R, D), BF16),
            DMA((2, NC)),
            DMA((2, NC)),
            DMA((2, NC)),
            DMA((2, NC)),
            DMA((NC,)),
            DMA((NC,)),
            DMA((2, NC)),
            DMA((2, NC)),
            DMA((NY, NZ)),
            DMA((NY, NZ)),
            DMA((NY, NZ)),
            DMA((NY, NZ)),
            DMA((NZ,)),
            DMA((NZ,)),
            DMA((4,)),
            DMA((4,)),
            pltpu.SemaphoreType.REGULAR,
        ],
        compiler_params=pltpu.CompilerParams(
            collective_id=0, has_side_effects=True, vmem_limit_bytes=40 * 1024 * 1024
        ),
    )(valid_rows, dest_shard[0], *[pltpu.with_memory_space_constraint(v, pltpu.HBM) for v in operands])


def solution(mesh):
    tiles = mesh.shape["tile"]
    NZ = min(8, max(1, tiles // 2))
    NY = tiles // NZ

    def local(points, valid_rows, dest_shard, dest_slot, ng, wxz, wbc, wdt, *params):
        wdt = jnp.transpose(wdt, (0, 2, 1))
        return call(NY, NZ, points, valid_rows, dest_shard, ng, wxz, wbc, wdt, *params)

    in_specs = (
        P("tile", "curve", None),
        P("tile", "curve"),
        P("tile", "curve", None),
        P("tile", "curve", None),
    ) + (P(),) * 9
    return jax.shard_map(
        local, mesh=mesh, in_specs=in_specs, out_specs=P("tile", "curve", None), check_vma=False
    )
```

```python
import functools

import jax
import jax.numpy as jnp
from jax import lax
from jax.experimental import pallas as pl
from jax.experimental.pallas import tpu as pltpu
from jax.sharding import PartitionSpec as P

F32 = jnp.float32
BF16 = jnp.bfloat16
HI = lax.Precision.HIGHEST
NC = 8
R = 128
D = 512
E = 1024
H = 16
CH = 512
W = 256
NX = E // W


def silu(v):
    return v * jax.nn.sigmoid(v)


def softplus(v):
    return jnp.maximum(v, 0.0) + jnp.log1p(jnp.exp(-jnp.abs(v)))


def mesh_copy(src, dst, send_sem, recv_sem, tile, curve):
    return pltpu.make_async_remote_copy(
        src_ref=src,
        dst_ref=dst,
        send_sem=send_sem,
        recv_sem=recv_sem,
        device_id=(tile, curve),
        device_id_type=pl.DeviceIdType.MESH,
    )


def kernel(
    NY,
    NZ,
    valid_v,
    dest_v,
    x_h,
    ng_h,
    wxz_h,
    wbc_h,
    wdt_h,
    dtb_h,
    rate_h,
    skip_h,
    gg_h,
    wout_h,
    out_h,
    x_v,
    ng,
    wxz,
    wbc,
    wdt,
    dtb,
    rate,
    skip,
    gg,
    wout,
    in_sem,
    exp_m,
    vals,
    gate,
    inner,
    decx,
    acc,
    ggx,
    sA,
    rA,
    lS,
    lR,
    iS,
    iR,
    sC,
    rC,
    pre,
    lpre,
    tS,
    tR,
    sB1,
    rB1,
    sB3,
    rB3,
    mS,
    mR,
    pS,
    pR,
    a_send,
    a_recv,
    l_send,
    l_recv,
    i_send,
    i_recv,
    c_send,
    c_recv,
    t_send,
    t_recv,
    b1_send,
    b1_recv,
    b3_send,
    b3_recv,
    m_send,
    m_recv,
    ready,
):
    t = lax.axis_index("tile")
    c = lax.axis_index("curve")
    y = t // NZ
    z = lax.rem(t, NZ)
    RZ = R // NZ
    curve_peer = [lax.rem(c + k, NC) for k in range(NC)]
    z_peer = [lax.rem(z + k, NZ) for k in range(NZ)]
    x = c // 2
    partner = c + 1 - 2 * lax.rem(c, 2)
    far_first = (4, 5, 3, 2, 6, 7, 1)

    barrier = pltpu.get_barrier_semaphore()

    def signal(sem, tile, curve):
        pl.semaphore_signal(
            sem, inc=1, device_id=(tile, curve), device_id_type=pl.DeviceIdType.MESH
        )

    def each_tile(first, last, sem):
        def one(i, _):
            signal(sem, i, c)
            return 0

        lax.fori_loop(first, last, one, 0)

    for k in range(1, NC):
        signal(barrier, t, curve_peer[k])
    each_tile(t + 1, NY * NZ, barrier)

    n_in = [0]

    def fetch(src, dst):
        cp = pltpu.make_async_copy(src, dst, in_sem.at[n_in[0]])
        n_in[0] += 1
        cp.start()
        return cp

    def fetch_xz(layer):
        return [
            fetch(wxz_h.at[layer, :, pl.ds(q * CH, CH)], wxz.at[layer, q])
            for q in range(2 * E // CH)
        ]

    small_cp = [fetch(a, b) for a, b in ((dtb_h, dtb), (rate_h, rate), (skip_h, skip))]
    x_cp = fetch(x_h.at[0], x_v)
    small_cp += [fetch(ng_h, ng)]
    dt_cp = [fetch(wdt_h.at[0], wdt.at[0])]
    xz_cp = [fetch_xz(0)]
    bc_cp = [fetch(wbc_h.at[0], wbc.at[0])]
    small_cp += [fetch(gg_h, gg)]
    out_cp = [fetch(wout_h.at[0], wout.at[0])]

    lane = lax.broadcasted_iota(jnp.int32, (R, R), 1)
    row = lax.broadcasted_iota(jnp.int32, (R, R), 0)
    row_f = row.astype(F32)
    causal = row >= lane
    tri = jnp.concatenate([jnp.where(causal, 1.0, 0.0).astype(BF16)] * 3, axis=1)
    for j in range(NC):
        exp_m[j // 2, :, (j % 2) * R : (j % 2 + 1) * R] = jnp.where(
            jnp.logical_and(row < 48, (row & 15) == (lane >> 6) + 2 * j), 1.0, 0.0
        ).astype(BF16)
    rep = jnp.where(
        lax.broadcasted_iota(jnp.int32, (H, R), 0)
        == (lax.broadcasted_iota(jnp.int32, (H, R), 1) & 15),
        1.0,
        0.0,
    )

    def parts_of(v):
        hi = v.astype(BF16).astype(F32)
        rest = v - hi
        mid = rest.astype(BF16).astype(F32)
        low = rest - mid
        ln = lax.broadcasted_iota(jnp.int32, v.shape, 1)
        return jnp.where(ln < 16, hi, jnp.where(ln < 32, mid, low)).astype(BF16)

    def widen(parts, q):
        return jnp.dot(parts, exp_m[q], preferred_element_type=F32)

    def copies8(v):
        return jnp.dot(v, rep, precision=HI, preferred_element_type=F32)


    def norm_of(xb, layer):
        w = xb.astype(F32)
        ms = jnp.mean(w * w, axis=-1, keepdims=True)
        return (w * lax.rsqrt(ms + 1e-05) * ng[layer : layer + 1, :]).astype(BF16)

    def times_of(nb, live, layer):
        wrep = jnp.concatenate([wdt[layer]] * 8, axis=0)
        raw = lax.dot_general(
            nb, wrep, (((1,), (1,)), ((), ())), preferred_element_type=F32
        )
        steps = softplus(raw + bias8[layer : layer + 1, :])
        steps = steps * live
        fall = -steps * rate8[layer : layer + 1, :]
        hi = fall.astype(BF16)
        rest = fall - hi.astype(F32)
        mid = rest.astype(BF16)
        low = (rest - mid.astype(F32)).astype(BF16)
        running = jnp.dot(
            tri, jnp.concatenate([hi, mid, low], axis=0), preferred_element_type=F32
        )
        return steps, running

    def project_values(nb, layer):
        for q in range(E // CH):
            v = silu(jnp.dot(nb, wxz[layer, q], preferred_element_type=F32)).astype(BF16)
            for i in range(CH // W):
                vals[q * (CH // W) + i] = v[:, i * W : (i + 1) * W]

    def project_gate(nb, layer):
        for q in range(E // CH):
            v = silu(jnp.dot(nb, wxz[layer, q + E // CH], preferred_element_type=F32))
            for i in range(CH // W):
                gate[q * (CH // W) + i] = v[:, i * W : (i + 1) * W]

    def keys_of(nb, layer):
        return silu(jnp.dot(nb, wbc[layer, :, 0:R], preferred_element_type=F32))

    def queries_of(nb, layer):
        return silu(jnp.dot(nb, wbc[layer, :, R : 2 * R], preferred_element_type=F32)).astype(BF16)

    sent = []

    def go(copy):
        copy.start()
        sent.append(copy)
        return copy

    def arrive(copies):
        for cp in copies:
            cp.wait_recv()

    def fill_logs(layer, running):
        total = parts_of(jnp.broadcast_to(running[R - 1 : R, :], (8, R)))
        for q in range(NX):
            wide = widen(total, q)
            lS[layer, 2 * q] = wide[0:1, :R]
            lS[layer, 2 * q + 1] = wide[0:1, R:]

    def send_logs(layer):
        got = []
        for k in far_first:
            got.append(
                go(
                    mesh_copy(
                        lS.at[layer, curve_peer[k]],
                        lR.at[layer, c],
                        l_send.at[layer, k],
                        l_recv.at[layer, k],
                        t,
                        curve_peer[k],
                    )
                )
            )
        lR[layer, c] = lS[layer, c]
        return got

    def make_states(layer, steps, running, keys):
        wide = parts_of(jnp.exp(running[R - 1 : R, :] - running) * steps)
        keys_t = keys.T.astype(BF16)

        for q in range(NX):
            scaled = (vals[q].astype(F32) * widen(wide, q)).astype(BF16)
            both = jnp.dot(keys_t, scaled, preferred_element_type=F32).astype(BF16)
            sA[layer, 2 * q] = both[:, :R]
            sA[layer, 2 * q + 1] = both[:, R:]

    def send_states(layer):
        got_l, got = send_logs(layer), []

        def send(j):
            k = lax.rem(j - c + NC, NC)
            got.append(
                go(
                    mesh_copy(
                        sA.at[layer, j],
                        rA.at[layer, c],
                        a_send.at[layer, k],
                        a_recv.at[layer, k],
                        t,
                        j,
                    )
                )
            )

        chip = [lax.rem(x + d, NX) for d in range(NX)]
        for d in (2, 1, 3):
            send(2 * chip[d])
            send(2 * chip[d] + 1)
        send(partner)
        rA[layer, c] = sA[layer, c]
        return got_l, got

    def carried_copy(layer, k):
        return mesh_copy(
            sC.at[layer, curve_peer[k]],
            rC.at[layer, c],
            c_send.at[layer, k],
            c_recv.at[layer, k],
            t,
            curve_peer[k],
        )

    def scores_of(keys, queries):
        scores = lax.dot_general(
            queries, keys.astype(BF16), (((1,), (1,)), ((), ())), preferred_element_type=F32
        )
        return jnp.where(causal, scores, 0.0)

    def inside(layer, steps_t, running, running_t, scores, which):
        half = lane < 64
        wide = parts_of(jnp.exp(running))
        for q in which:
            decx[q] = widen(wide, q)
            skips = widen(skip_parts, q)[layer : layer + 1, :]
            for j in (2 * q, 2 * q + 1):
                cols = slice((j % 2) * R, (j % 2 + 1) * R)
                vf = vals[q, :, cols].astype(F32)
                ws, ves = [], []
                for e in range(2):
                    h = 2 * j + e
                    gap = running[:, h : h + 1] - running_t[h : h + 1, :]
                    w = jnp.exp(jnp.minimum(gap, 0.0)) * steps_t[h : h + 1, :] * scores
                    ve = jnp.where(half if e == 0 else jnp.logical_not(half), vf, 0.0)
                    ws.append(w.astype(BF16))
                    ves.append(ve.astype(BF16))
                inner[q, :, cols] = skips[:, cols] * vf + jnp.dot(
                    jnp.concatenate(ws, axis=1),
                    jnp.concatenate(ves, axis=0),
                    preferred_element_type=F32,
                )

    def finish(layer, xb, live_col, queries):
        squares = jnp.zeros((R, W), F32)
        for d in (0, 1, 3, 2):
            xs = lax.rem(x + 4 - d, 4)
            both = (2 * xs, 2 * xs + 1)
            for src in (partner,) if d == 0 else both:
                mesh_copy(
                    sC.at[layer, src],
                    rC.at[layer, src],
                    c_send.at[layer, 0],
                    c_recv.at[layer, lax.rem(c - src + NC, NC)],
                    t,
                    src,
                ).wait_recv()
            states = jnp.concatenate([rC[layer, both[0]], rC[layer, both[1]]], axis=1)
            from_state = jnp.dot(queries, states, preferred_element_type=F32)
            g = (inner[xs] + decx[xs] * from_state) * gate[xs]
            squares = squares + g * g
            block = (g * ggx[layer, xs]).astype(BF16)
            rows = pl.ds(pl.multiple_of(xs * (2 * R), 2 * R), 2 * R)
            new = jnp.dot(block, wout[layer, rows, :], preferred_element_type=F32)
            if d == 0:
                acc[...] = new
            elif d != 2:
                acc[...] += new
        scale = lax.rsqrt(jnp.sum(squares, axis=-1, keepdims=True) * (1.0 / E) + 1e-05)
        update = acc[...] + new
        return (xb.astype(F32) + (live_col * scale) * update).astype(BF16)

    for cp in small_cp[:3]:
        cp.wait()
    valid_row = jnp.broadcast_to(valid_v[...], (1, R)).astype(F32)
    iS[0:1, :] = jnp.broadcast_to(dest_v[...], (1, R)).astype(F32)
    iS[1:2, :] = valid_row
    live = jnp.where(row_f < valid_row, 1.0, 0.0)
    bias8, rate8 = copies8(dtb[...]), copies8(rate[...])
    skip_parts = parts_of(jnp.concatenate([copies8(skip[...])] * 4, axis=0))
    x_cp.wait()
    small_cp[3].wait()
    xb = x_v[...]
    nb = norm_of(xb, 0)
    for cp in (dt_cp[0], bc_cp[0], xz_cp[0][0], xz_cp[0][1]):
        cp.wait()
    steps, running = times_of(nb, live, 0)
    keys = keys_of(nb, 0)
    project_values(nb, 0)
    fill_logs(0, running)
    make_states(0, steps, running, keys)
    pl.semaphore_wait(barrier, (NC - 1) + t)
    got_l, got = send_states(0)
    got_i = []
    for k in far_first:
        got_i.append(
            go(mesh_copy(iS, iR.at[c], i_send.at[k], i_recv.at[k], t, curve_peer[k]))
        )
    iR[c] = iS[...]
    each_tile(0, t, ready)
    small_cp[4].wait()
    for layer in range(2):
        for q in range(NX):
            ggx[layer, q] = gg[layer : layer + 1, q * W : (q + 1) * W]
    dt_cp.append(fetch(wdt_h.at[1], wdt.at[1]))
    bc_cp.append(fetch(wbc_h.at[1], wbc.at[1]))
    xz_cp.append(fetch_xz(1))
    out_cp.append(fetch(wout_h.at[1], wout.at[1]))
    xz_cp[0][2].wait()
    xz_cp[0][3].wait()
    project_gate(nb, 0)
    queries = queries_of(nb, 0)
    scores = scores_of(keys, queries)
    running_t, steps_t = running.T, steps.T
    arrive(got_l)
    arrive(got)
    state = jnp.zeros((R, R), F32)
    for p in range(NC):
        sC[0, p] = state.astype(BF16)
        if p < NC - 1:
            state = jnp.exp(lR[0, p]) * state + rA[0, p].astype(F32)
    got = [go(carried_copy(0, k)) for k in far_first]
    rC[0, c] = sC[0, c]
    inside(0, steps_t, running, running_t, scores, range(NX))
    out_cp[0].wait()
    dt_cp[1].wait()
    bc_cp[1].wait()
    for cp in xz_cp[1]:
        cp.wait()
    out_cp[1].wait()
    arrive(got_i)
    first = finish(0, xb, live[:, 0:1], queries)
    mS[...] = first

    nb = norm_of(first, 1)
    steps, running = times_of(nb, live, 1)
    keys = keys_of(nb, 1)
    project_values(nb, 1)
    fill_logs(1, running)
    make_states(1, steps, running, keys)
    got_l, got_a = send_states(1)

    got_m = []
    for k in (1, 3, 2):
        got_m.append(
            go(mesh_copy(mS, mR.at[k], m_send.at[k], m_recv.at[k], t, curve_peer[2 * k]))
        )

    far_z = (4, 3, 5, 2, 6, 1, 7, 0) if NZ == 8 else tuple(range(NZ))

    def row_sends(start_copy):
        own = [start_copy(0, k) for k in far_z if k > 0]
        later = [[start_copy(a, k) for k in far_z] for a in range(1, NY)]
        for a in (2, 1, 3) if NY == 4 else range(1, NY):
            cps = later[a - 1]

            @pl.when(y + a < NY)
            def _():
                for cp in cps:
                    cp.start()

        for cp in own:
            cp.start()
        return own, later

    def row_arrive(pair):
        own, later = pair
        arrive(own)
        for a in range(1, NY):

            @pl.when(y >= a)
            def _():
                arrive(later[a - 1])

    def row_sent(pair):
        own, later = pair
        for cp in own:
            cp.wait_send()
        for a in range(1, NY):

            @pl.when(y + a < NY)
            def _():
                for cp in later[a - 1]:
                    cp.wait_send()

    arrive(got_l)
    logs = [lR[1, s] for s in range(NC)]
    place = [iR[s, 0:1, :] for s in range(NC)]
    tile_log = logs[0]
    for s in range(1, NC):
        tile_log = tile_log + logs[s]
    tS[...] = tile_log
    weights = []
    for s in range(NC):
        after = jnp.zeros((1, R), F32)
        for o in range(NC):
            if o != s:
                after = after + jnp.where(place[o] > place[s], logs[o], 0.0)
        weights.append(jnp.exp(after))
    tR[y, z] = tile_log

    @pl.when(t < NY * NZ - 1)
    def _():
        pl.semaphore_wait(ready, NY * NZ - 1 - t)

    logs_sent = row_sends(
        lambda a, k: mesh_copy(
            tS,
            tR.at[y, z],
            t_send.at[a, k],
            t_recv.at[a, k],
            (y + a) * NZ + z_peer[k],
            c,
        )
    )
    arrive(got_a)
    total = weights[0] * rA[1, 0].astype(F32)
    for s in range(1, NC):
        total = total + weights[s] * rA[1, s].astype(F32)
    for k in range(NZ):
        sB1[k] = total[k * RZ : (k + 1) * RZ, :].astype(BF16)
    rB1[y, z] = sB1[z]
    states_sent = row_sends(
        lambda a, k: mesh_copy(
            sB1.at[z_peer[k]],
            rB1.at[y, z],
            b1_send.at[a, k],
            b1_recv.at[a, k],
            (y + a) * NZ + z_peer[k],
            c,
        )
    )

    def lap(p, carry):
        state, log_sum = carry
        pre[p] = state
        lpre[p] = log_sum
        pf = p.astype(F32)
        here = [jnp.where(place[s] == pf, 1.0, 0.0) for s in range(NC)]
        log_p = here[0] * logs[0]
        new = here[0] * rA[1, 0].astype(F32)
        for s in range(1, NC):
            log_p = log_p + here[s] * logs[s]
            new = new + here[s] * rA[1, s].astype(F32)
        return jnp.exp(log_p) * state + new, log_sum + log_p

    lax.fori_loop(0, NC, lap, (jnp.zeros((R, R), F32), jnp.zeros((1, R), F32)))

    row_arrive(logs_sent)
    row_arrive(states_sent)
    state = jnp.zeros((RZ, R), F32)
    for a in range(NY - 1):
        new = state
        for k in range(NZ):
            new = jnp.exp(tR[a, k]) * new + rB1[a, k].astype(F32)
        state = jnp.where(a < y, new, state)
    for k in range(NZ):
        sB3[k] = state.astype(BF16)
        if k < NZ - 1:
            state = jnp.exp(tR[y, k]) * state + rB1[y, k].astype(F32)
    rB3[z] = sB3[z]
    got = []
    for k in [k for k in far_z if k > 0]:
        got.append(
            go(
                mesh_copy(
                    sB3.at[z_peer[k]],
                    rB3.at[z],
                    b3_send.at[k],
                    b3_recv.at[k],
                    y * NZ + z_peer[k],
                    c,
                )
            )
        )
    arrive(got_m)
    c_f, partner_f = c.astype(F32), partner.astype(F32)
    mine = jnp.zeros((R, D), F32)
    theirs = jnp.zeros((R, D), F32)
    for k in range(4):
        goes = iR[lax.rem(c + NC - 2 * k, NC), 0:1, :]
        blk = (mS[...] if k == 0 else mR[k]).astype(F32)
        m_mine = jnp.concatenate([jnp.where(goes == c_f, 1.0, 0.0)] * 4, axis=1)
        m_theirs = jnp.concatenate([jnp.where(goes == partner_f, 1.0, 0.0)] * 4, axis=1)
        mine = mine + m_mine * blk
        theirs = theirs + m_theirs * blk
    pS[...] = theirs.astype(BF16)
    x_v[...] = mine.astype(BF16)
    valid_row = jnp.zeros((1, R), F32)
    for s in range(NC):
        valid_row = valid_row + jnp.where(place[s] == c_f, 1.0, 0.0) * iR[s, 1:2, :]
    live = jnp.where(row_f < valid_row, 1.0, 0.0)
    swap = go(mesh_copy(pS, pR, m_send.at[0], m_recv.at[0], t, partner))

    swap.wait_recv()
    xb = (x_v[...].astype(F32) + pR[...].astype(F32)).astype(BF16)
    nb = norm_of(xb, 1)
    steps, running = times_of(nb, live, 1)
    keys = keys_of(nb, 1)
    queries = queries_of(nb, 1)
    project_values(nb, 1)

    project_gate(nb, 1)
    scores = scores_of(keys, queries)
    running_t, steps_t = running.T, steps.T
    arrive(got)
    entry = jnp.concatenate([rB3[k].astype(F32) for k in range(NZ)], axis=0)
    got, ready = [], None
    for k in far_first:
        p = curve_peer[k]
        sC[1, p] = (jnp.exp(lpre[p]) * entry + pre[p]).astype(BF16)
        if ready is not None:
            got.append(go(ready))
        ready = carried_copy(1, k)
    rC[1, c] = (jnp.exp(lpre[c]) * entry + pre[c]).astype(BF16)
    got.append(go(ready))
    inside(1, steps_t, running, running_t, scores, range(NX))
    last = {id(cp) for cp in got}
    for cp in sent:
        if id(cp) not in last:
            cp.wait_send()
    row_sent(logs_sent)
    row_sent(states_sent)
    out_h[0] = finish(1, xb, live[:, 0:1], queries)
    for cp in got:
        cp.wait_send()


def call(NY, NZ, points, valid_rows, dest_shard, *params):
    RZ = R // NZ
    operands = (points, *params)
    V = pltpu.VMEM
    DMA = pltpu.SemaphoreType.DMA
    hbm = pl.BlockSpec(memory_space=pltpu.HBM)
    vmem = pl.BlockSpec(memory_space=pltpu.VMEM)
    return pl.pallas_call(
        functools.partial(kernel, NY, NZ),
        out_shape=jax.ShapeDtypeStruct(points.shape, points.dtype),
        in_specs=[vmem, vmem] + [hbm] * 10,
        out_specs=pl.BlockSpec(memory_space=pltpu.VMEM),
        scratch_shapes=[
            V((R, D), BF16),
            V((2, D), F32),
            V((2, 2 * E // CH, D, CH), BF16),
            V((2, D, 2 * R), BF16),
            V((2, H, D), BF16),
            V((2, H), F32),
            V((2, H), F32),
            V((2, H), F32),
            V((2, E), F32),
            V((2, E, D), BF16),
            DMA((20,)),
            V((NX, R, W), BF16),
            V((NX, R, W), BF16),
            V((NX, R, W), F32),
            V((NX, R, W), F32),
            V((NX, R, W), F32),
            V((R, D), F32),
            V((2, NX, 1, W), F32),
            V((2, NC, R, R), BF16),
            V((2, NC, R, R), BF16),
            V((2, NC, 1, R), F32),
            V((2, NC, 1, R), F32),
            V((2, R), F32),
            V((NC, 2, R), F32),
            V((2, NC, R, R), BF16),
            V((2, NC, R, R), BF16),
            V((NC, R, R), F32),
            V((NC, 1, R), F32),
            V((1, R), F32),
            V((NY, NZ, 1, R), F32),
            V((NZ, RZ, R), BF16),
            V((NY, NZ, RZ, R), BF16),
            V((NZ, RZ, R), BF16),
            V((NZ, RZ, R), BF16),
            V((R, D), BF16),
            V((4, R, D), BF16),
            V((R, D), BF16),
            V((R, D), BF16),
            DMA((2, NC)),
            DMA((2, NC)),
            DMA((2, NC)),
            DMA((2, NC)),
            DMA((NC,)),
            DMA((NC,)),
            DMA((2, NC)),
            DMA((2, NC)),
            DMA((NY, NZ)),
            DMA((NY, NZ)),
            DMA((NY, NZ)),
            DMA((NY, NZ)),
            DMA((NZ,)),
            DMA((NZ,)),
            DMA((4,)),
            DMA((4,)),
            pltpu.SemaphoreType.REGULAR,
        ],
        compiler_params=pltpu.CompilerParams(
            collective_id=0, has_side_effects=True, vmem_limit_bytes=40 * 1024 * 1024
        ),
    )(valid_rows, dest_shard[0], *[pltpu.with_memory_space_constraint(v, pltpu.HBM) for v in operands])


def solution(mesh):
    tiles = mesh.shape["tile"]
    NZ = min(8, max(1, tiles // 2))
    NY = tiles // NZ

    def local(points, valid_rows, dest_shard, dest_slot, ng, wxz, wbc, wdt, *params):
        wdt = jnp.transpose(wdt, (0, 2, 1))
        return call(NY, NZ, points, valid_rows, dest_shard, ng, wxz, wbc, wdt, *params)

    in_specs = (
        P("tile", "curve", None),
        P("tile", "curve"),
        P("tile", "curve", None),
        P("tile", "curve", None),
    ) + (P(),) * 9
    return jax.shard_map(
        local, mesh=mesh, in_specs=in_specs, out_specs=P("tile", "curve", None), check_vma=False
    )
```

```python
import functools

import jax
import jax.numpy as jnp
from jax import lax
from jax.experimental import pallas as pl
from jax.experimental.pallas import tpu as pltpu
from jax.sharding import PartitionSpec as P

F32 = jnp.float32
BF16 = jnp.bfloat16
HI = lax.Precision.HIGHEST
NC = 8
R = 128
D = 512
E = 1024
H = 16
CH = 512
W = 256
NX = E // W


def silu(v):
    return v * jax.nn.sigmoid(v)


def softplus(v):
    return jnp.maximum(v, 0.0) + jnp.log1p(jnp.exp(-jnp.abs(v)))


def mesh_copy(src, dst, send_sem, recv_sem, tile, curve):
    return pltpu.make_async_remote_copy(
        src_ref=src,
        dst_ref=dst,
        send_sem=send_sem,
        recv_sem=recv_sem,
        device_id=(tile, curve),
        device_id_type=pl.DeviceIdType.MESH,
    )


def kernel(
    NY,
    NZ,
    valid_v,
    dest_v,
    x_h,
    ng_h,
    wxz_h,
    wbc_h,
    wdt_h,
    dtb_h,
    rate_h,
    skip_h,
    gg_h,
    wout_h,
    out_h,
    x_v,
    ng,
    wxz,
    wbc,
    wdt,
    dtb,
    rate,
    skip,
    gg,
    wout,
    in_sem,
    exp_m,
    vals,
    gate,
    inner,
    decx,
    acc,
    ggx,
    sA,
    rA,
    lS,
    lR,
    iS,
    iR,
    sC,
    rC,
    pre,
    lpre,
    tS,
    tR,
    sB1,
    rB1,
    sB3,
    rB3,
    mS,
    mR,
    pS,
    pR,
    a_send,
    a_recv,
    l_send,
    l_recv,
    i_send,
    i_recv,
    c_send,
    c_recv,
    t_send,
    t_recv,
    b1_send,
    b1_recv,
    b3_send,
    b3_recv,
    m_send,
    m_recv,
    ready,
):
    t = lax.axis_index("tile")
    c = lax.axis_index("curve")
    y = t // NZ
    z = lax.rem(t, NZ)
    RZ = R // NZ
    curve_peer = [lax.rem(c + k, NC) for k in range(NC)]
    z_peer = [lax.rem(z + k, NZ) for k in range(NZ)]
    x = c // 2
    partner = c + 1 - 2 * lax.rem(c, 2)
    far_first = (4, 5, 3, 2, 6, 7, 1)

    barrier = pltpu.get_barrier_semaphore()

    def signal(sem, tile, curve):
        pl.semaphore_signal(
            sem, inc=1, device_id=(tile, curve), device_id_type=pl.DeviceIdType.MESH
        )

    def each_tile(first, last, sem):
        def one(i, _):
            signal(sem, i, c)
            return 0

        lax.fori_loop(first, last, one, 0)

    for k in range(1, NC):
        signal(barrier, t, curve_peer[k])
    each_tile(t + 1, NY * NZ, barrier)

    n_in = [0]

    def fetch(src, dst):
        cp = pltpu.make_async_copy(src, dst, in_sem.at[n_in[0]])
        n_in[0] += 1
        cp.start()
        return cp

    def fetch_xz(layer):
        return [
            fetch(wxz_h.at[layer, :, pl.ds(q * CH, CH)], wxz.at[layer, q])
            for q in range(2 * E // CH)
        ]

    small_cp = [fetch(a, b) for a, b in ((dtb_h, dtb), (rate_h, rate), (skip_h, skip))]
    x_cp = fetch(x_h.at[0], x_v)
    small_cp += [fetch(ng_h, ng)]
    dt_cp = [fetch(wdt_h.at[0], wdt.at[0])]
    xz_cp = [fetch_xz(0)]
    bc_cp = [fetch(wbc_h.at[0], wbc.at[0])]
    small_cp += [fetch(gg_h, gg)]
    out_cp = [fetch(wout_h.at[0], wout.at[0])]

    lane = lax.broadcasted_iota(jnp.int32, (R, R), 1)
    row = lax.broadcasted_iota(jnp.int32, (R, R), 0)
    row_f = row.astype(F32)
    causal = row >= lane
    tri = jnp.concatenate([jnp.where(causal, 1.0, 0.0).astype(BF16)] * 3, axis=1)
    for j in range(NC):
        exp_m[j // 2, :, (j % 2) * R : (j % 2 + 1) * R] = jnp.where(
            jnp.logical_and(row < 48, (row & 15) == (lane >> 6) + 2 * j), 1.0, 0.0
        ).astype(BF16)
    rep = jnp.where(
        lax.broadcasted_iota(jnp.int32, (H, R), 0)
        == (lax.broadcasted_iota(jnp.int32, (H, R), 1) & 15),
        1.0,
        0.0,
    )

    def parts_of(v):
        hi = v.astype(BF16).astype(F32)
        rest = v - hi
        mid = rest.astype(BF16).astype(F32)
        low = rest - mid
        ln = lax.broadcasted_iota(jnp.int32, v.shape, 1)
        return jnp.where(ln < 16, hi, jnp.where(ln < 32, mid, low)).astype(BF16)

    def widen(parts, q):
        return jnp.dot(parts, exp_m[q], preferred_element_type=F32)

    def copies8(v):
        return jnp.dot(v, rep, precision=HI, preferred_element_type=F32)


    def norm_of(xb, layer):
        w = xb.astype(F32)
        ms = jnp.mean(w * w, axis=-1, keepdims=True)
        return (w * lax.rsqrt(ms + 1e-05) * ng[layer : layer + 1, :]).astype(BF16)

    def times_of(nb, live, layer):
        wrep = jnp.concatenate([wdt[layer]] * 8, axis=0)
        raw = lax.dot_general(
            nb, wrep, (((1,), (1,)), ((), ())), preferred_element_type=F32
        )
        steps = softplus(raw + bias8[layer : layer + 1, :])
        steps = steps * live
        fall = -steps * rate8[layer : layer + 1, :]
        hi = fall.astype(BF16)
        rest = fall - hi.astype(F32)
        mid = rest.astype(BF16)
        low = (rest - mid.astype(F32)).astype(BF16)
        running = jnp.dot(
            tri, jnp.concatenate([hi, mid, low], axis=0), preferred_element_type=F32
        )
        return steps, running

    def project_values(nb, layer):
        for q in range(E // CH):
            v = silu(jnp.dot(nb, wxz[layer, q], preferred_element_type=F32)).astype(BF16)
            for i in range(CH // W):
                vals[q * (CH // W) + i] = v[:, i * W : (i + 1) * W]

    def project_gate(nb, layer):
        for q in range(E // CH):
            v = silu(jnp.dot(nb, wxz[layer, q + E // CH], preferred_element_type=F32))
            for i in range(CH // W):
                gate[q * (CH // W) + i] = v[:, i * W : (i + 1) * W]

    def keys_of(nb, layer):
        return silu(jnp.dot(nb, wbc[layer, :, 0:R], preferred_element_type=F32))

    def queries_of(nb, layer):
        return silu(jnp.dot(nb, wbc[layer, :, R : 2 * R], preferred_element_type=F32)).astype(BF16)

    sent = []

    def go(copy):
        copy.start()
        sent.append(copy)
        return copy

    def arrive(copies):
        for cp in copies:
            cp.wait_recv()

    def fill_logs(layer, running):
        total = parts_of(jnp.broadcast_to(running[R - 1 : R, :], (8, R)))
        for q in range(NX):
            wide = widen(total, q)
            lS[layer, 2 * q] = wide[0:1, :R]
            lS[layer, 2 * q + 1] = wide[0:1, R:]

    def send_logs(layer):
        got = []
        for k in far_first:
            got.append(
                go(
                    mesh_copy(
                        lS.at[layer, curve_peer[k]],
                        lR.at[layer, c],
                        l_send.at[layer, k],
                        l_recv.at[layer, k],
                        t,
                        curve_peer[k],
                    )
                )
            )
        lR[layer, c] = lS[layer, c]
        return got

    def make_states(layer, steps, running, keys):
        wide = parts_of(jnp.exp(running[R - 1 : R, :] - running) * steps)
        keys_t = keys.T.astype(BF16)

        for q in range(NX):
            scaled = (vals[q].astype(F32) * widen(wide, q)).astype(BF16)
            both = jnp.dot(keys_t, scaled, preferred_element_type=F32).astype(BF16)
            sA[layer, 2 * q] = both[:, :R]
            sA[layer, 2 * q + 1] = both[:, R:]

    def send_states(layer):
        got_l, got = send_logs(layer), []

        def send(j):
            k = lax.rem(j - c + NC, NC)
            got.append(
                go(
                    mesh_copy(
                        sA.at[layer, j],
                        rA.at[layer, c],
                        a_send.at[layer, k],
                        a_recv.at[layer, k],
                        t,
                        j,
                    )
                )
            )

        chip = [lax.rem(x + d, NX) for d in range(NX)]
        for d in (2, 1, 3):
            send(2 * chip[d])
            send(2 * chip[d] + 1)
        send(partner)
        rA[layer, c] = sA[layer, c]
        return got_l, got

    def carried_copy(layer, k):
        return mesh_copy(
            sC.at[layer, curve_peer[k]],
            rC.at[layer, c],
            c_send.at[layer, k],
            c_recv.at[layer, k],
            t,
            curve_peer[k],
        )

    def scores_of(keys, queries):
        scores = lax.dot_general(
            queries, keys.astype(BF16), (((1,), (1,)), ((), ())), preferred_element_type=F32
        )
        return jnp.where(causal, scores, 0.0)

    def inside(layer, steps_t, running, running_t, scores, which):
        half = lane < 64
        wide = parts_of(jnp.exp(running))
        for q in which:
            decx[q] = widen(wide, q)
            skips = widen(skip_parts, q)[layer : layer + 1, :]
            for j in (2 * q, 2 * q + 1):
                cols = slice((j % 2) * R, (j % 2 + 1) * R)
                vf = vals[q, :, cols].astype(F32)
                ws, ves = [], []
                for e in range(2):
                    h = 2 * j + e
                    gap = running[:, h : h + 1] - running_t[h : h + 1, :]
                    w = jnp.exp(jnp.minimum(gap, 0.0)) * steps_t[h : h + 1, :] * scores
                    ve = jnp.where(half if e == 0 else jnp.logical_not(half), vf, 0.0)
                    ws.append(w.astype(BF16))
                    ves.append(ve.astype(BF16))
                inner[q, :, cols] = skips[:, cols] * vf + jnp.dot(
                    jnp.concatenate(ws, axis=1),
                    jnp.concatenate(ves, axis=0),
                    preferred_element_type=F32,
                )

    def finish(layer, xb, live_col, queries):
        squares = jnp.zeros((R, W), F32)
        for d in (0, 1, 3, 2):
            xs = lax.rem(x + 4 - d, 4)
            both = (2 * xs, 2 * xs + 1)
            for src in (partner,) if d == 0 else both:
                mesh_copy(
                    sC.at[layer, src],
                    rC.at[layer, src],
                    c_send.at[layer, 0],
                    c_recv.at[layer, lax.rem(c - src + NC, NC)],
                    t,
                    src,
                ).wait_recv()
            states = jnp.concatenate([rC[layer, both[0]], rC[layer, both[1]]], axis=1)
            from_state = jnp.dot(queries, states, preferred_element_type=F32)
            g = (inner[xs] + decx[xs] * from_state) * gate[xs]
            squares = squares + g * g
            block = (g * ggx[layer, xs]).astype(BF16)
            rows = pl.ds(pl.multiple_of(xs * (2 * R), 2 * R), 2 * R)
            new = jnp.dot(block, wout[layer, rows, :], preferred_element_type=F32)
            if d == 0:
                acc[...] = new
            elif d != 2:
                acc[...] += new
        scale = lax.rsqrt(jnp.sum(squares, axis=-1, keepdims=True) * (1.0 / E) + 1e-05)
        update = acc[...] + new
        return (xb.astype(F32) + (live_col * scale) * update).astype(BF16)

    for cp in small_cp[:3]:
        cp.wait()
    valid_row = jnp.broadcast_to(valid_v[...], (1, R)).astype(F32)
    iS[0:1, :] = jnp.broadcast_to(dest_v[...], (1, R)).astype(F32)
    iS[1:2, :] = valid_row
    live = jnp.where(row_f < valid_row, 1.0, 0.0)
    bias8, rate8 = copies8(dtb[...]), copies8(rate[...])
    skip_parts = parts_of(jnp.concatenate([copies8(skip[...])] * 4, axis=0))
    x_cp.wait()
    small_cp[3].wait()
    xb = x_v[...]
    nb = norm_of(xb, 0)
    for cp in (dt_cp[0], bc_cp[0], xz_cp[0][0], xz_cp[0][1]):
        cp.wait()
    steps, running = times_of(nb, live, 0)
    keys = keys_of(nb, 0)
    project_values(nb, 0)
    fill_logs(0, running)
    make_states(0, steps, running, keys)
    pl.semaphore_wait(barrier, (NC - 1) + t)
    got_l, got = send_states(0)
    got_i = []
    for k in far_first:
        got_i.append(
            go(mesh_copy(iS, iR.at[c], i_send.at[k], i_recv.at[k], t, curve_peer[k]))
        )
    iR[c] = iS[...]
    each_tile(0, t, ready)
    small_cp[4].wait()
    for layer in range(2):
        for q in range(NX):
            ggx[layer, q] = gg[layer : layer + 1, q * W : (q + 1) * W]
    dt_cp.append(fetch(wdt_h.at[1], wdt.at[1]))
    bc_cp.append(fetch(wbc_h.at[1], wbc.at[1]))
    xz_cp.append(fetch_xz(1))
    out_cp.append(fetch(wout_h.at[1], wout.at[1]))
    xz_cp[0][2].wait()
    xz_cp[0][3].wait()
    project_gate(nb, 0)
    queries = queries_of(nb, 0)
    scores = scores_of(keys, queries)
    running_t, steps_t = running.T, steps.T
    arrive(got_l)
    arrive(got)
    state = jnp.zeros((R, R), F32)
    for p in range(NC):
        sC[0, p] = state.astype(BF16)
        if p < NC - 1:
            state = jnp.exp(lR[0, p]) * state + rA[0, p].astype(F32)
    got = [go(carried_copy(0, k)) for k in far_first]
    rC[0, c] = sC[0, c]
    inside(0, steps_t, running, running_t, scores, range(NX))
    out_cp[0].wait()
    dt_cp[1].wait()
    bc_cp[1].wait()
    for cp in xz_cp[1]:
        cp.wait()
    out_cp[1].wait()
    arrive(got_i)
    first = finish(0, xb, live[:, 0:1], queries)
    mS[...] = first

    nb = norm_of(first, 1)
    steps, running = times_of(nb, live, 1)
    keys = keys_of(nb, 1)
    project_values(nb, 1)
    fill_logs(1, running)
    make_states(1, steps, running, keys)
    got_l, got_a = send_states(1)

    got_m = []
    for k in (1, 3, 2):
        got_m.append(
            go(mesh_copy(mS, mR.at[k], m_send.at[k], m_recv.at[k], t, curve_peer[2 * k]))
        )

    far_z = (4, 3, 5, 2, 6, 1, 7, 0) if NZ == 8 else tuple(range(NZ))

    def row_sends(start_copy):
        own = [start_copy(0, k) for k in far_z if k > 0]
        later = [[start_copy(a, k) for k in far_z] for a in range(1, NY)]
        for a in (2, 1, 3) if NY == 4 else range(1, NY):
            cps = later[a - 1]

            @pl.when(y + a < NY)
            def _():
                for cp in cps:
                    cp.start()

        for cp in own:
            cp.start()
        return own, later

    def row_arrive(pair):
        own, later = pair
        arrive(own)
        for a in range(1, NY):

            @pl.when(y >= a)
            def _():
                arrive(later[a - 1])

    def row_sent(pair):
        own, later = pair
        for cp in own:
            cp.wait_send()
        for a in range(1, NY):

            @pl.when(y + a < NY)
            def _():
                for cp in later[a - 1]:
                    cp.wait_send()

    arrive(got_l)
    logs = [lR[1, s] for s in range(NC)]
    place = [iR[s, 0:1, :] for s in range(NC)]
    tile_log = logs[0]
    for s in range(1, NC):
        tile_log = tile_log + logs[s]
    tS[...] = tile_log
    weights = []
    for s in range(NC):
        after = jnp.zeros((1, R), F32)
        for o in range(NC):
            if o != s:
                after = after + jnp.where(place[o] > place[s], logs[o], 0.0)
        weights.append(jnp.exp(after))
    tR[y, z] = tile_log

    @pl.when(t < NY * NZ - 1)
    def _():
        pl.semaphore_wait(ready, NY * NZ - 1 - t)

    logs_sent = row_sends(
        lambda a, k: mesh_copy(
            tS,
            tR.at[y, z],
            t_send.at[a, k],
            t_recv.at[a, k],
            (y + a) * NZ + z_peer[k],
            c,
        )
    )
    arrive(got_a)
    total = weights[0] * rA[1, 0].astype(F32)
    for s in range(1, NC):
        total = total + weights[s] * rA[1, s].astype(F32)
    for k in range(NZ):
        sB1[k] = total[k * RZ : (k + 1) * RZ, :].astype(BF16)
    rB1[y, z] = sB1[z]
    states_sent = row_sends(
        lambda a, k: mesh_copy(
            sB1.at[z_peer[k]],
            rB1.at[y, z],
            b1_send.at[a, k],
            b1_recv.at[a, k],
            (y + a) * NZ + z_peer[k],
            c,
        )
    )

    def lap(p, carry):
        state, log_sum = carry
        pre[p] = state
        lpre[p] = log_sum
        pf = p.astype(F32)
        here = [jnp.where(place[s] == pf, 1.0, 0.0) for s in range(NC)]
        log_p = here[0] * logs[0]
        new = here[0] * rA[1, 0].astype(F32)
        for s in range(1, NC):
            log_p = log_p + here[s] * logs[s]
            new = new + here[s] * rA[1, s].astype(F32)
        return jnp.exp(log_p) * state + new, log_sum + log_p

    lax.fori_loop(0, NC, lap, (jnp.zeros((R, R), F32), jnp.zeros((1, R), F32)))

    row_arrive(logs_sent)
    row_arrive(states_sent)
    state = jnp.zeros((RZ, R), F32)
    for a in range(NY - 1):
        new = state
        for k in range(NZ):
            new = jnp.exp(tR[a, k]) * new + rB1[a, k].astype(F32)
        state = jnp.where(a < y, new, state)
    for k in range(NZ):
        sB3[k] = state.astype(BF16)
        if k < NZ - 1:
            state = jnp.exp(tR[y, k]) * state + rB1[y, k].astype(F32)
    rB3[z] = sB3[z]
    got = []
    for k in [k for k in far_z if k > 0]:
        got.append(
            go(
                mesh_copy(
                    sB3.at[z_peer[k]],
                    rB3.at[z],
                    b3_send.at[k],
                    b3_recv.at[k],
                    y * NZ + z_peer[k],
                    c,
                )
            )
        )
    arrive(got_m)
    c_f, partner_f = c.astype(F32), partner.astype(F32)
    mine = jnp.zeros((R, D), F32)
    theirs = jnp.zeros((R, D), F32)
    for k in range(4):
        goes = iR[lax.rem(c + NC - 2 * k, NC), 0:1, :]
        blk = (mS[...] if k == 0 else mR[k]).astype(F32)
        m_mine = jnp.concatenate([jnp.where(goes == c_f, 1.0, 0.0)] * 4, axis=1)
        m_theirs = jnp.concatenate([jnp.where(goes == partner_f, 1.0, 0.0)] * 4, axis=1)
        mine = mine + m_mine * blk
        theirs = theirs + m_theirs * blk
    pS[...] = theirs.astype(BF16)
    x_v[...] = mine.astype(BF16)
    valid_row = jnp.zeros((1, R), F32)
    for s in range(NC):
        valid_row = valid_row + jnp.where(place[s] == c_f, 1.0, 0.0) * iR[s, 1:2, :]
    live = jnp.where(row_f < valid_row, 1.0, 0.0)
    swap = go(mesh_copy(pS, pR, m_send.at[0], m_recv.at[0], t, partner))

    swap.wait_recv()
    xb = (x_v[...].astype(F32) + pR[...].astype(F32)).astype(BF16)
    nb = norm_of(xb, 1)
    steps, running = times_of(nb, live, 1)
    keys = keys_of(nb, 1)
    queries = queries_of(nb, 1)
    project_values(nb, 1)

    arrive(got)
    entry = jnp.concatenate([rB3[k].astype(F32) for k in range(NZ)], axis=0)
    got, ready = [], None
    for k in far_first:
        p = curve_peer[k]
        sC[1, p] = (jnp.exp(lpre[p]) * entry + pre[p]).astype(BF16)
        if ready is not None:
            got.append(go(ready))
        ready = carried_copy(1, k)
    rC[1, c] = (jnp.exp(lpre[c]) * entry + pre[c]).astype(BF16)
    got.append(go(ready))
    project_gate(nb, 1)
    scores = scores_of(keys, queries)
    running_t, steps_t = running.T, steps.T
    inside(1, steps_t, running, running_t, scores, range(NX))
    last = {id(cp) for cp in got}
    for cp in sent:
        if id(cp) not in last:
            cp.wait_send()
    row_sent(logs_sent)
    row_sent(states_sent)
    out_h[0] = finish(1, xb, live[:, 0:1], queries)
    for cp in got:
        cp.wait_send()


def call(NY, NZ, points, valid_rows, dest_shard, *params):
    RZ = R // NZ
    operands = (points, *params)
    V = pltpu.VMEM
    DMA = pltpu.SemaphoreType.DMA
    hbm = pl.BlockSpec(memory_space=pltpu.HBM)
    vmem = pl.BlockSpec(memory_space=pltpu.VMEM)
    return pl.pallas_call(
        functools.partial(kernel, NY, NZ),
        out_shape=jax.ShapeDtypeStruct(points.shape, points.dtype),
        in_specs=[vmem, vmem] + [hbm] * 10,
        out_specs=pl.BlockSpec(memory_space=pltpu.VMEM),
        scratch_shapes=[
            V((R, D), BF16),
            V((2, D), F32),
            V((2, 2 * E // CH, D, CH), BF16),
            V((2, D, 2 * R), BF16),
            V((2, H, D), BF16),
            V((2, H), F32),
            V((2, H), F32),
            V((2, H), F32),
            V((2, E), F32),
            V((2, E, D), BF16),
            DMA((20,)),
            V((NX, R, W), BF16),
            V((NX, R, W), BF16),
            V((NX, R, W), F32),
            V((NX, R, W), F32),
            V((NX, R, W), F32),
            V((R, D), F32),
            V((2, NX, 1, W), F32),
            V((2, NC, R, R), BF16),
            V((2, NC, R, R), BF16),
            V((2, NC, 1, R), F32),
            V((2, NC, 1, R), F32),
            V((2, R), F32),
            V((NC, 2, R), F32),
            V((2, NC, R, R), BF16),
            V((2, NC, R, R), BF16),
            V((NC, R, R), F32),
            V((NC, 1, R), F32),
            V((1, R), F32),
            V((NY, NZ, 1, R), F32),
            V((NZ, RZ, R), BF16),
            V((NY, NZ, RZ, R), BF16),
            V((NZ, RZ, R), BF16),
            V((NZ, RZ, R), BF16),
            V((R, D), BF16),
            V((4, R, D), BF16),
            V((R, D), BF16),
            V((R, D), BF16),
            DMA((2, NC)),
            DMA((2, NC)),
            DMA((2, NC)),
            DMA((2, NC)),
            DMA((NC,)),
            DMA((NC,)),
            DMA((2, NC)),
            DMA((2, NC)),
            DMA((NY, NZ)),
            DMA((NY, NZ)),
            DMA((NY, NZ)),
            DMA((NY, NZ)),
            DMA((NZ,)),
            DMA((NZ,)),
            DMA((4,)),
            DMA((4,)),
            pltpu.SemaphoreType.REGULAR,
        ],
        compiler_params=pltpu.CompilerParams(
            collective_id=0, has_side_effects=True, vmem_limit_bytes=40 * 1024 * 1024
        ),
    )(valid_rows, dest_shard[0], *[pltpu.with_memory_space_constraint(v, pltpu.HBM) for v in operands])


def solution(mesh):
    tiles = mesh.shape["tile"]
    NZ = min(8, max(1, tiles // 2))
    NY = tiles // NZ

    def local(points, valid_rows, dest_shard, dest_slot, ng, wxz, wbc, wdt, *params):
        wdt = jnp.transpose(wdt, (0, 2, 1))
        return call(NY, NZ, points, valid_rows, dest_shard, ng, wxz, wbc, wdt, *params)

    in_specs = (
        P("tile", "curve", None),
        P("tile", "curve"),
        P("tile", "curve", None),
        P("tile", "curve", None),
    ) + (P(),) * 9
    return jax.shard_map(
        local, mesh=mesh, in_specs=in_specs, out_specs=P("tile", "curve", None), check_vma=False
    )
```
